32 devices in a mesh: sc: 4 (over y, x), rows: 8 (over z, core).
Axes of the slice: x: 2, y: 2, z: 4, core: 2. Of those that a mesh axis runs over, the one named last changes fastest.
Arguments:
- embeddings: bfloat16 [32768, 1024], P(('sc', 'rows')), may hold values from -6 to 6
- labels: int32 [32768, 1], P(('sc', 'rows')), may hold values from 0 to 3; in each aligned block of 1024 rows (0 to 1023, 1024 to 2047, ...) at most 512 rows name the same one
- init_idx: int32 [4, 256], P('sc'), may hold values from 0 to 16383
Outputs:
- assign: bfloat16 [32768, 256], P(('sc', 'rows'))
- centroids: float32 [4, 256, 1024], P('sc')
The draws below stay inside these ranges and needn't reach their ends.
Inputs may be any that keep to these rules, and one draw needn't show every extreme that they name: `labels`: among the rows of one device (aligned blocks of 1024 rows) no label occurs more than 512 times, and some label occurs exactly 512 times; every label occurs somewhere.
All inputs are finite; a program needn't handle non-finite values.
Results may differ from the reference program's by a relative error of at most 0.0052.
Values may be sent and summed in bfloat16 or wider, within the bound.
A program may use at most 64 MiB of HBM per device.

```python
import math
import jax
import jax.numpy as jnp
import numpy as np
from jax import lax

E = 1024
K = 256
TOK_DEV = 1024
ITERS = 3
ROUNDS = 3
SUPER = 4
CAP = 512
ROWS_ALL = 32768
DEVICES = 32


def draw_embeddings(key, part):
    centre_key = jax.random.fold_in(key, 101)
    block_key = jax.random.fold_in(key, 202)
    pick_key = jax.random.fold_in(key, 303)
    noise_key = jax.random.fold_in(key, 404)
    centre_count = 96
    block_count = ROWS_ALL // TOK_DEV
    centres = jax.random.normal(centre_key, (centre_count, E), jnp.float32)
    block_dirs = jax.random.normal(block_key, (block_count, E), jnp.float32)
    pick = jax.random.randint(pick_key, (ROWS_ALL,), 0, centre_count)
    block_of = jnp.arange(ROWS_ALL, dtype=jnp.int32) // TOK_DEV
    noise = jax.random.normal(noise_key, (ROWS_ALL, E), jnp.float32)
    values = centres[pick] + 0.8 * block_dirs[block_of] + 0.4 * noise
    return jnp.clip(values, -6.0, 6.0).astype(jnp.bfloat16)


def set_ends(drawn, key, low, top_value):
    dims = drawn.shape
    index_at = [jax.random.randint(jax.random.fold_in(key, axis), (), 0, dims[axis]) for axis in range(len(dims))]
    drawn = drawn.at[tuple(index_at)].set(low)
    longest = dims.index(max(dims))
    index_at[longest] = (index_at[longest] + 1) % dims[longest]
    return drawn.at[tuple(index_at)].set(top_value)


def shared_out(own_key, own, number, rows, count, top, reach, slope):
    order = jax.random.permutation(own_key, count)
    heavy_load, usual = load_shares(count, rows * top, reach, slope, True), load_shares(count, rows * top, reach, slope, False)
    places = jnp.arange(count)

    def named(sizes, offset_by):
        used = int((sizes > 0).sum())
        fixed = max(1, used // 4)
        shifted = fixed + (places - fixed + offset_by * (used - fixed)) % max(1, count - fixed)
        return jnp.zeros((count,), jnp.int32).at[order[jnp.where(places < fixed, places, shifted)]].set(jnp.asarray(sizes, jnp.int32))

    sizes = jnp.where(number % 4 == 0, named(heavy_load, number // 4), named(usual, number - number // 4 - 1))
    mixed = jax.random.permutation(jax.random.fold_in(own, 3), count)
    donor, taker = mixed[0:count // 2 * 2:2], mixed[1:count // 2 * 2:2]
    slack = jnp.minimum(sizes[donor] - 1, reach - sizes[taker]) // 2
    slack = jnp.where((donor == order[0]) | (taker == order[0]) | (sizes[taker] == 0), 0, jnp.maximum(slack, 0))
    shifted = jax.random.randint(jax.random.fold_in(own, 4), (count // 2,), 0, 1 << 20) % (slack + 1)
    sizes = sizes.at[donor].add(-shifted).at[taker].add(shifted)
    items = jnp.searchsorted(jnp.cumsum(sizes), jnp.arange(rows * top), side="right").astype(jnp.int32)
    listing = items.reshape(top, rows).T
    listing = listing[jax.random.permutation(jax.random.fold_in(own, 1), rows)]
    offset_by = jax.random.randint(jax.random.fold_in(own, 2), (rows, 1), 0, top)
    return jnp.take_along_axis(listing, (jnp.arange(top)[None, :] + offset_by) % top, axis=1)


def load_shares(amount, total, limit, slope, full):
    weights = [(1 << 20) // math.isqrt(grade ** slope) + 1 for grade in range(1, amount + 1)]
    largest = limit if full else min(limit, max(-(-total // amount), total * weights[0] // sum(weights)))
    least = 1 if total - largest >= amount - 1 else 0
    holding, surplus = [largest] + [least] * (amount - 1), total - largest - least * (amount - 1)
    while surplus > 0:
        candidates = [i for i in range(1, amount) if holding[i] < largest] or [i for i in range(1, amount) if holding[i] < limit]
        whole, remaining = sum([weights[i] for i in candidates]), surplus
        for i in candidates:
            addition = min(limit - holding[i], max(1, remaining * weights[i] // whole), surplus)
            holding[i] = holding[i] + addition
            surplus = surplus - addition
    return np.array(holding)


def setup_inputs(seed: int = 0) -> dict:
    seeds = jax.random.split(jax.random.key(seed), 4)
    embeddings = draw_embeddings(jax.random.fold_in(seeds[3], 71), 0)
    labels_keys = jax.random.split(jax.random.fold_in(seeds[1], 1), ROWS_ALL // TOK_DEV)
    labels_turns = jax.random.permutation(jax.random.fold_in(seeds[1], 3), ROWS_ALL // TOK_DEV)
    labels = jax.vmap(lambda own, number: shared_out(jax.random.fold_in(seeds[1], 2), own, number, TOK_DEV, SUPER, 1, CAP, 2))(labels_keys, labels_turns).reshape((ROWS_ALL, 1))
    init_idx = set_ends(jax.random.randint(seeds[2], (SUPER, K), 0, DEVICES * CAP), jax.random.fold_in(seeds[2], 1), 0, (DEVICES * CAP) - 1).astype(jnp.int32)
    return {"embeddings": embeddings, "labels": labels, "init_idx": init_idx}


def unit_of(rows):
    values = rows.astype(jnp.float32)
    scale = lax.rsqrt(lax.optimization_barrier(jnp.mean(values * values, axis=1, keepdims=True)) + 1e-05) * (1.0 / math.sqrt(rows.shape[1]))
    return (values * scale).astype(jnp.bfloat16)

def balance(plan, valid):
    for step in range(ITERS):
        plan = plan / lax.optimization_barrier(jnp.sum(plan, axis=0))[None, :]
        row_sum = lax.optimization_barrier(jnp.sum(plan, axis=1))
        plan = jnp.where(valid[:, None], plan / jnp.where(valid, row_sum, 1.0)[:, None], 0.0)
    return plan

def run_rounds(members, valid, cent):
    for round_index in range(ROUNDS):
        scores = jnp.dot(members, cent.T, preferred_element_type=jnp.float32)
        plan = jnp.where(valid[:, None], jnp.exp(scores * 10.0), 0.0)
        plan = balance(plan, valid)
        plan_b = plan.astype(jnp.bfloat16)
        mass = jnp.dot(plan_b.T, members, preferred_element_type=jnp.float32)
        if round_index < ROUNDS - 1:
            cent = (mass * lax.rsqrt(lax.optimization_barrier(jnp.sum(mass * mass, axis=1, keepdims=True)) + 1e-06)).astype(jnp.bfloat16)
        else:
            means = mass / lax.optimization_barrier(jnp.sum(plan, axis=0))[:, None]
    return (means, plan)

def reference(embeddings, labels, init_idx):
    label_col = labels[:, 0]
    total_rows = label_col.shape[0]
    unit_rows = unit_of(embeddings)
    order = jnp.argsort(label_col, stable=True).astype(jnp.int32)
    member = (label_col[:, None] == jnp.arange(SUPER, dtype=jnp.int32)[None, :]).astype(jnp.int32)
    counts = lax.optimization_barrier(jnp.sum(member, axis=0))
    starts = jnp.cumsum(counts) - counts
    longest = DEVICES * CAP

    def one_group(assign, group):
        count = counts[group]
        offsets = jnp.arange(longest, dtype=jnp.int32)
        valid = offsets < count
        index = order[jnp.clip(starts[group] + offsets, 0, total_rows - 1)]
        members = jnp.where(valid[:, None], unit_rows[index], jnp.zeros_like(unit_rows[index]))
        wanted = init_idx[group] % count
        cent = members[wanted]
        means, plan = run_rounds(members, valid, cent)
        target = jnp.where(valid, index, total_rows)
        assign = assign.at[target].set(plan.astype(jnp.bfloat16), mode='drop')
        return (assign, means)
    start_assign = jnp.zeros((total_rows, K), jnp.bfloat16)
    assign, centroids = lax.scan(one_group, start_assign, jnp.arange(SUPER, dtype=jnp.int32))
    return (assign, centroids)
```

```python
import functools
import math

import jax
import jax.numpy as jnp
from jax import lax
from jax.experimental import pallas as pl
from jax.experimental.pallas import tpu as pltpu
from jax.sharding import PartitionSpec as P

ITERS = 3
ROUNDS = 3
MESH = pl.DeviceIdType.MESH
F32 = jnp.float32
BF16 = jnp.bfloat16


def kernel(
    G, R, tok, E, K, S, T,
    x_ref, labr_ref, init_ref,
    assign_ref, means_ref,
    xu, out, inc, plan, planb, lhst, acc, ret, target,
    cnt, cntr, cs, s1s, s1r, s2s, s2r, cent,
    d_ss, d_rs, c_ss, c_rs, k_ss, k_rs, cs_ss, cs_rs,
    s1_ss, s1_rs, s2_ss, s2_rs, g_ss, g_rs, f_ss, f_rs, r_ss, r_rs,
):
    g = lax.axis_index("sc")
    r = lax.axis_index("rows")
    Z = R // 2
    H = K // 2
    Q = H // Z
    M = 2 if Q % 32 == 0 else 1
    QM = Q // M
    N = G * S
    z = r // 2
    c = r % 2
    oc = 1 - c
    partner = z * 2 + oc

    def copy(src, dst, ss, rs, to):
        return pltpu.make_async_remote_copy(
            src_ref=src, dst_ref=dst, send_sem=ss, recv_sem=rs,
            device_id=to, device_id_type=MESH,
        )

    barrier = pltpu.get_barrier_semaphore()
    for off in range(1, R):
        pl.semaphore_signal(barrier, inc=1, device_id=(g, (r + off) % R), device_id_type=MESH)
    for off in range(1, G):
        pl.semaphore_signal(barrier, inc=1, device_id=((g + off) % G, r), device_id_type=MESH)

    def unit(i, carry):
        at = pl.ds(pl.multiple_of(i * 128, 128), 128)
        v = x_ref[at, :].astype(F32)
        scale = lax.rsqrt(jnp.mean(v * v, axis=1, keepdims=True) + 1e-05) * (1.0 / math.sqrt(E))
        xu[at, :] = (v * scale).astype(BF16)
        return carry

    lax.fori_loop(0, tok // 128, unit, 0)

    labr = labr_ref[...]
    sub = lax.broadcasted_iota(jnp.int32, (128, 128), 0)
    lane = lax.broadcasted_iota(jnp.int32, (128, 128), 1)
    tri = jnp.where(sub < lane, 1.0, 0.0).astype(BF16)
    mem = jnp.where(lax.broadcasted_iota(jnp.int32, (16, tok), 0) == labr, 1.0, 0.0)
    seen = jnp.zeros((16, 1), F32)
    places = []
    for b in range(tok // 128):
        part = mem[:, b * 128:(b + 1) * 128]
        before = jnp.dot(part.astype(BF16), tri, preferred_element_type=F32) + seen
        places.append(jnp.sum(before * part, axis=0, keepdims=True))
        seen = seen + jnp.sum(part, axis=1, keepdims=True)
    place_i = jnp.concatenate(places, axis=1).astype(jnp.int32)
    cnt[g] = jnp.sum(jnp.where(sub[:16] == lane[:16], seen, 0.0), axis=0, keepdims=True)

    pl.semaphore_wait(barrier, R - 1 + G - 1)

    count_sends = []
    for off in range(1, G):
        to = (g + off) % G
        d = copy(cnt.at[g], cnt.at[g], c_ss.at[off], c_rs.at[g], (to, r))
        d.start()
        count_sends.append(d)

    DT = min(128, S)
    per = S // DT
    row_sends = []
    chosen = [jnp.where(labr == (g + off) % G, place_i, -1) for off in range(1, G + 1)]
    for j, off in [(j, off) for j in range(per) for off in range(1, G)] + [(j, G) for j in range(per)]:
        at = pl.ds(j * DT, DT)
        slot = lax.broadcasted_iota(jnp.int32, (DT, tok), 0) + j * DT
        perm = jnp.where(slot == chosen[off - 1], 1.0, 0.0).astype(BF16)
        block = jnp.dot(perm, xu[...], preferred_element_type=F32).astype(BF16)
        if off < G:
            out[off - 1, at, :] = block
            d = copy(
                out.at[off - 1, at, :], inc.at[g, at, :],
                d_ss.at[off * per + j], d_rs.at[g * per + j], ((g + off) % G, r),
            )
            d.start()
            row_sends.append(d)
        else:
            inc[g, at, :] = block

    slot_of = (labr * S + place_i).astype(F32)
    for b in range(tok // 128):
        wide = jnp.broadcast_to(slot_of[:, b * 128:(b + 1) * 128], (128, 128))
        target[pl.ds(b * 128, 128), :] = wide.T[:, :1].astype(jnp.int32)

    for off in range(1, G):
        src = (g + off) % G
        copy(cnt.at[src], cnt.at[src], c_ss.at[off], c_rs.at[src], (src, r)).wait_recv()
    lanes = lax.broadcasted_iota(jnp.int32, (1, 128), 1)
    mine = jnp.zeros((1, 128), F32)
    n_here = []
    for q in range(G):
        n_q = jnp.sum(jnp.where(lanes == g, cnt[q], 0.0), axis=1, keepdims=True)
        n_here.append(n_q)
        mine = mine + jnp.where(lanes == q, n_q, 0.0)
    cntr[r] = mine
    rank_sends = []
    for off in range(1, R):
        to = (r + off) % R
        d = copy(cntr.at[r], cntr.at[r], k_ss.at[off], k_rs.at[r], (g, to))
        d.start()
        rank_sends.append(d)
    for off in range(1, R):
        src = (r + off) % R
        copy(cntr.at[src], cntr.at[src], k_ss.at[off], k_rs.at[src], (g, src)).wait_recv()
    total = jnp.zeros((1, 128), F32)
    early = jnp.zeros((1, 128), F32)
    for q in range(R):
        row = cntr[q]
        total = total + row
        early = early + jnp.where(r > q, row, 0.0)
    count = jnp.sum(total, axis=1, keepdims=True)
    asked = jnp.broadcast_to(init_ref[...].astype(F32), (128, K)).T[:, :1]
    wanted = asked - jnp.floor((asked + 0.5) / count) * count
    slots = lax.broadcasted_iota(jnp.int32, (1, S), 1).astype(F32)
    for q in range(G):
        base = jnp.sum(
            jnp.where(lanes < q, total, 0.0) + jnp.where(lanes == q, early, 0.0),
            axis=1, keepdims=True,
        )
        rank = jnp.where(slots < n_here[q], slots + base, -1.0)
        pick = jnp.where(wanted == rank, 1.0, 0.0).astype(BF16)
        lhst[0, :, pl.ds(q * S, S)] = pick[:H]
        lhst[1, :, pl.ds(q * S, S)] = pick[H:]

    for off in range(1, G):
        src = (g + off) % G
        for j in range(per):
            part = inc.at[src, pl.ds(j * DT, DT), :]
            copy(part, part, d_ss.at[off * per + j], d_rs.at[src * per + j], (src, r)).wait_recv()

    C = E // 2

    def half_sum(h, e):
        rows = inc[:, :, pl.ds(e * C, C)].reshape(N, C)
        return jnp.dot(lhst[h], rows, preferred_element_type=F32)

    def big(t, finish, meanwhile=None):
        slot = t % 2
        first = []
        sends = []
        for e in range(2):
            s1s[e] = half_sum(oc, e).astype(BF16)
            d = copy(s1s.at[e], s1r.at[slot, e], s1_ss.at[slot, e], s1_rs.at[slot, e], (g, partner))
            d.start()
            first.append(d)
        for e in range(2):
            acc[e] = half_sum(c, e)
        for d in first:
            d.wait_recv()
        for m in range(M):
            at = pl.ds(m * Z * QM, Z * QM)
            for e in range(2):
                both = acc[e, at, :] + s1r[slot, e, at, :].astype(F32)
                acc[e, at, :] = both
                s2s[m, :, :, pl.ds(e * C, C)] = both.astype(BF16).reshape(Z, QM, C)
            for off in range(1, Z):
                to = (z + off) % Z
                d = copy(
                    s2s.at[m, to], s2r.at[slot, m, z],
                    s2_ss.at[slot, m, off], s2_rs.at[slot, m, z], (g, to * 2 + c),
                )
                d.start()
                sends.append(d)
        for m in range(M):
            at = pl.ds(pl.multiple_of(m * Z * QM + z * QM, QM), QM)
            own = jnp.concatenate([acc[0, at, :], acc[1, at, :]], axis=1)
            for off in range(1, Z):
                src = (z + off) % Z
                part = s2r.at[slot, m, src]
                copy(
                    part, part, s2_ss.at[slot, m, off], s2_rs.at[slot, m, src], (g, src * 2 + c)
                ).wait_recv()
                own = own + s2r[slot, m, src].astype(F32)
            mine = cent.at[slot, c, m, z]
            cent[slot, c, m, z] = finish(own, m).astype(BF16)
            for off in range(1, Z):
                to = (z + off) % Z
                d = copy(mine, mine, g_ss.at[slot, m, off], g_rs.at[slot, m, z], (g, to * 2 + c))
                d.start()
                sends.append(d)
            d = copy(mine, mine, f_ss.at[slot, m, z], f_rs.at[slot, m, z], (g, partner))
            d.start()
            sends.append(d)
        if meanwhile is not None:
            meanwhile()
        for m in range(M):
            for off in range(1, Z):
                src = (z + off) % Z
                part = cent.at[slot, c, m, src]
                copy(part, part, g_ss.at[slot, m, off], g_rs.at[slot, m, src], (g, src * 2 + c)).wait_recv()
                d = copy(part, part, f_ss.at[slot, m, src], f_rs.at[slot, m, src], (g, partner))
                d.start()
                sends.append(d)
        for m in range(M):
            for off in range(Z):
                src = (z + off) % Z
                part = cent.at[slot, oc, m, src]
                copy(part, part, f_ss.at[slot, m, src], f_rs.at[slot, m, src], (g, partner)).wait_recv()
        for d in first + sends:
            d.wait_send()

    def column_start(t, part8):
        slot = t % 2
        cs[slot, r] = jnp.sum(part8, axis=0, keepdims=True)
        sends = []
        for off in sorted(range(1, R), key=lambda o: -min(o, R - o)):
            to = (r + off) % R
            d = copy(cs.at[slot, r], cs.at[slot, r], cs_ss.at[slot, off], cs_rs.at[slot, r], (g, to))
            d.start()
            sends.append(d)
        return sends

    def column_sum(t, sends):
        slot = t % 2
        for off in range(1, R):
            src = (r + off) % R
            part = cs.at[slot, src]
            copy(part, part, cs_ss.at[slot, off], cs_rs.at[slot, src], (g, src)).wait_recv()
        whole = cs[slot, 0]
        for q in range(1, R):
            whole = whole + cs[slot, q]
        for d in sends:
            d.wait_send()
        return whole

    tiles = N // T
    zero8 = jnp.zeros((8, K), F32)

    def down(v):
        return jnp.sum(v.reshape(T // 8, 8, K), axis=0)

    def assign_rows():
        for off in range(1, G):
            src = (g + off) % G
            part = ret.at[src]
            copy(part, part, r_ss.at[off], r_rs.at[src], (src, r)).wait_recv()

        def one(i, carry):
            at = pl.ds(pl.multiple_of(i * 256, 256), 256)
            hot = jnp.where(
                lax.broadcasted_iota(jnp.int32, (256, N), 1) == target[at, :], 1.0, 0.0
            ).astype(BF16)
            assign_ref[at, :] = jnp.dot(
                hot, ret[...].reshape(N, K), preferred_element_type=F32
            ).astype(BF16)
            return carry

        lax.fori_loop(0, tok // 256, one, 0)

    big(0, lambda v, m: v)
    step = 0
    back_sends = []
    valid = [
        (lax.broadcasted_iota(jnp.int32, (S, 1), 0)).astype(F32) < n_here[q] for q in range(G)
    ]
    for round_index in range(ROUNDS):
        last = round_index == ROUNDS - 1
        slot = round_index % 2
        part = zero8
        for i in range(tiles):
            at = pl.ds(i * T, T)
            q, first = i * T // S, i * T % S
            v = lax.dot_general(
                inc[q, pl.ds(first, T), :], cent[slot].reshape(K, E),
                (((1,), (1,)), ((), ())), preferred_element_type=F32,
            )
            v = jnp.where(valid[q][first:first + T], jnp.exp(v * 10.0), 0.0)
            plan[at, :] = v
            part = part + down(v)
        for it in range(ITERS):
            col = 1.0 / column_sum(step, column_start(step, part))
            step += 1
            part = zero8
            for i in range(tiles):
                at = pl.ds(i * T, T)
                v = plan[at, :] * col
                s = jnp.sum(v, axis=1, keepdims=True)
                u = jnp.where(s > 0.0, 1.0 / s, 0.0)
                if it < ITERS - 1:
                    part = part + down(plan[at, :] * u)
                else:
                    v = v * u
                    if last:
                        planb[at, :] = v.astype(BF16)
                        part = part + down(v)
                    vt = v.T.astype(BF16)
                    lhst[0, :, at] = vt[:H]
                    lhst[1, :, at] = vt[H:]
        if not last:
            big(
                round_index + 1,
                lambda v, m: v * lax.rsqrt(jnp.sum(v * v, axis=1, keepdims=True) + 1e-06),
            )
        else:
            for off in range(1, G):
                to = (g + off) % G
                d = copy(
                    planb.at[pl.ds(pl.multiple_of(to * S, S), S), :], ret.at[g],
                    r_ss.at[off], r_rs.at[g], (to, r),
                )
                d.start()
                back_sends.append(d)
            ret[g] = planb[pl.ds(pl.multiple_of(g * S, S), S), :]
            weight_sends = column_start(step, part)
            weights = []

            def mean_of(v, m):
                if m == 0:
                    weights.append(column_sum(step, weight_sends))
                wide = lax.broadcasted_iota(jnp.int32, (QM, K), 0) + (c * H + m * Z * QM + z * QM)
                pick = wide == lax.broadcasted_iota(jnp.int32, (QM, K), 1)
                return v / jnp.sum(jnp.where(pick, weights[0], 0.0), axis=1, keepdims=True)

            big(ROUNDS, mean_of, assign_rows)
            means_ref[...] = cent[ROUNDS % 2].reshape(K, E).astype(F32)

    for d in count_sends + row_sends + rank_sends + back_sends:
        d.wait_send()


def on_device(G, R, embeddings, labels, init_idx):
    tok, E = embeddings.shape
    K = init_idx.shape[1]
    S = 2 * tok // G
    T = min(256, S)
    N = G * S
    Z = R // 2
    Q = K // 2 // Z
    M = 2 if Q % 32 == 0 else 1
    QM = Q // M
    per = S // min(128, S)
    dma = pltpu.SemaphoreType.DMA
    vm = pltpu.VMEM
    assign, means = pl.pallas_call(
        functools.partial(kernel, G, R, tok, E, K, S, T),
        out_shape=(
            jax.ShapeDtypeStruct((tok, K), BF16),
            jax.ShapeDtypeStruct((K, E), F32),
        ),
        in_specs=[pl.BlockSpec(memory_space=pltpu.VMEM)] * 3,
        out_specs=[pl.BlockSpec(memory_space=pltpu.VMEM)] * 2,
        scratch_shapes=[
            vm((tok, E), BF16),
            vm((G - 1, S, E), BF16),
            vm((G, S, E), BF16),
            vm((N, K), F32),
            vm((N, K), BF16),
            vm((2, K // 2, N), BF16),
            vm((2, K // 2, E // 2), F32),
            vm((G, S, K), BF16),
            vm((tok, 1), jnp.int32),
            vm((G, 1, 128), F32),
            vm((R, 1, 128), F32),
            vm((2, R, 1, K), F32),
            vm((2, K // 2, E // 2), BF16),
            vm((2, 2, K // 2, E // 2), BF16),
            vm((M, Z, QM, E), BF16),
            vm((2, M, Z, QM, E), BF16),
            vm((2, 2, M, Z, QM, E), BF16),
            dma(((G + 1) * per,)), dma((G * per,)),
            dma((G,)), dma((G,)),
            dma((R,)), dma((R,)),
            dma((2, R)), dma((2, R)),
            dma((2, 2)), dma((2, 2)),
            dma((2, M, Z)), dma((2, M, Z)),
            dma((2, M, Z)), dma((2, M, Z)),
            dma((2, M, Z)), dma((2, M, Z)),
            dma((G,)), dma((G,)),
        ],
        compiler_params=pltpu.CompilerParams(
            collective_id=0, has_side_effects=True, vmem_limit_bytes=48 * 1024 * 1024,
        ),
    )(embeddings, labels.reshape(1, tok), init_idx)
    return (assign, means[None])


def solution(mesh):
    return jax.shard_map(
        functools.partial(on_device, mesh.shape["sc"], mesh.shape["rows"]),
        mesh=mesh,
        in_specs=(P(("sc", "rows"), None), P(("sc", "rows"), None), P("sc", None)),
        out_specs=(P(("sc", "rows"), None), P("sc", None, None)),
        check_vma=False,
    )
```

```python
import functools
import math

import jax
import jax.numpy as jnp
from jax import lax
from jax.experimental import pallas as pl
from jax.experimental.pallas import tpu as pltpu
from jax.sharding import PartitionSpec as P

ITERS = 3
ROUNDS = 3
MESH = pl.DeviceIdType.MESH
F32 = jnp.float32
BF16 = jnp.bfloat16


def x_sem_rows(tok):
    return min(256, tok)


def cut(first, last, size):
    return [(at, min(size, last - at)) for at in range(first, last, size)]


def kernel(
    G, R, tok, E, K, S, T, A, pieces, early_pieces,
    x_ref, labr_ref, init_ref,
    assign_ref, means_ref,
    xin, xu, out, inc, plan, planb, lhst, acc, ret, target,
    msg, tab, cs, s1s, s1r, s2s, s2r, cent,
    x_sem, d_ss, d_rs, c_ss, c_rs, k_ss, k_rs, cs_ss, cs_rs,
    s1_ss, s1_rs, s2_ss, s2_rs, g_ss, g_rs, f_ss, f_rs, r_ss, r_rs,
):
    g = lax.axis_index("sc")
    r = lax.axis_index("rows")
    Z = R // 2
    H = K // 2
    Q = H // Z
    M = 2 if Q % 32 == 0 else 1
    QM = Q // M
    N = G * S
    GP = -(-G // 8) * 8
    F = pieces[early_pieces - 1][0] + pieces[early_pieces - 1][1]
    per = len(pieces)
    XT = x_sem_rows(tok)
    z = r // 2
    c = r % 2
    oc = 1 - c
    partner = z * 2 + oc

    def copy(src, dst, ss, rs, to):
        return pltpu.make_async_remote_copy(
            src_ref=src, dst_ref=dst, send_sem=ss, recv_sem=rs,
            device_id=to, device_id_type=MESH,
        )

    barrier = pltpu.get_barrier_semaphore()
    for off in range(1, R):
        pl.semaphore_signal(barrier, inc=1, device_id=(g, (r + off) % R), device_id_type=MESH)
    for off in range(1, G):
        pl.semaphore_signal(barrier, inc=1, device_id=((g + off) % G, r), device_id_type=MESH)

    for i in range(tok // XT):
        at = pl.ds(i * XT, XT)
        pltpu.make_async_copy(x_ref.at[at, :], xin.at[at, :], x_sem.at[i]).start()

    lanes = lax.broadcasted_iota(jnp.int32, (1, 128), 1)
    sub = lax.broadcasted_iota(jnp.int32, (128, 128), 0)
    lane = lax.broadcasted_iota(jnp.int32, (128, 128), 1)
    tri = jnp.where(sub < lane, 1.0, 0.0).astype(BF16)
    labr = labr_ref[...]
    mem = jnp.where(lax.broadcasted_iota(jnp.int32, (16, tok), 0) == labr, 1.0, 0.0)

    def before(marks):
        seen = jnp.zeros((16, 1), F32)
        places = []
        for b in range(tok // 128):
            part = marks[:, b * 128:(b + 1) * 128]
            ahead = jnp.dot(part.astype(BF16), tri, preferred_element_type=F32) + seen
            places.append(jnp.sum(ahead * mem[:, b * 128:(b + 1) * 128], axis=0, keepdims=True))
            seen = seen + jnp.sum(part, axis=1, keepdims=True)
        return jnp.concatenate(places, axis=1), seen

    place, held = before(mem)
    msg[g] = jnp.zeros((8, 128), F32)
    msg[g, 0:1, :] = jnp.sum(jnp.where(sub[:16] == lane[:16], held, 0.0), axis=0, keepdims=True)
    for i in range(K // 128):
        msg[g, 1 + i:2 + i, :] = init_ref[:, i * 128:(i + 1) * 128].astype(F32)

    pl.semaphore_wait(barrier, R - 1 + G - 1)

    count_sends = []
    for off in range(1, G):
        d = copy(msg.at[g], msg.at[g], c_ss.at[off], c_rs.at[g], ((g + off) % G, r))
        d.start()
        count_sends.append(d)

    for i in range(tok // XT):
        at = pl.ds(i * XT, XT)
        pltpu.make_async_copy(x_ref.at[at, :], xin.at[at, :], x_sem.at[i]).wait()
        v = xin[at, :].astype(F32)
        scale = lax.rsqrt(jnp.mean(v * v, axis=1, keepdims=True) + 1e-05) * (1.0 / math.sqrt(E))
        xu[at, :] = (v * scale).astype(BF16)

    row_sends = []

    def moved(chosen, start, size):
        slot = lax.broadcasted_iota(jnp.int32, (size, tok), 0) + start
        perm = jnp.concatenate([jnp.where(slot == one, 1.0, 0.0).astype(BF16) for one in chosen], axis=0)
        return jnp.dot(perm, xu[...], preferred_element_type=F32).astype(BF16)

    def send_piece(j, chosen):
        start, size = pieces[j]
        at = pl.ds(start, size)
        block = moved(chosen, start, size)
        for off in range(1, G):
            out[off - 1, at, :] = block[(off - 1) * size:off * size]
            d = copy(
                out.at[off - 1, at, :], inc.at[g, at, :],
                d_ss.at[off * per + j], d_rs.at[g * per + j], ((g + off) % G, r),
            )
            d.start()
            row_sends.append(d)

    def wait_piece(j):
        for off in range(1, G):
            src = (g + off) % G
            part = inc.at[src, pl.ds(*pieces[j]), :]
            copy(part, part, d_ss.at[off * per + j], d_rs.at[src * per + j], (src, r)).wait_recv()

    def chosen_of(place_i):
        return [jnp.where(labr == (g + off) % G, place_i, -1) for off in range(1, G + 1)]

    send_piece(0, chosen_of(place.astype(jnp.int32))[:G - 1])

    for off in range(1, G):
        src = (g + off) % G
        copy(msg.at[src], msg.at[src], c_ss.at[off], c_rs.at[src], (src, r)).wait_recv()
    tab[r] = jnp.zeros((GP, 128), F32)
    for q in range(G):
        tab[r, q:q + 1, :] = msg[q, 0:1, :]
    rank_sends = []
    for off in range(1, R):
        to = (r + off) % R
        d = copy(tab.at[r], tab.at[r], k_ss.at[off], k_rs.at[r], (g, to))
        d.start()
        rank_sends.append(d)
    for off in range(1, R):
        src = (r + off) % R
        copy(tab.at[src], tab.at[src], k_ss.at[off], k_rs.at[src], (g, src)).wait_recv()
    totals = jnp.zeros((GP, 128), F32)
    early = jnp.zeros((GP, 128), F32)
    for q in range(R):
        rows = tab[q]
        totals = totals + rows
        early = early + jnp.where(r > q, rows, 0.0)
    total = jnp.sum(totals, axis=0, keepdims=True)
    where_g = lax.broadcasted_iota(jnp.int32, (GP, 128), 0)
    ahead = jnp.sum(
        jnp.where(where_g < g, totals, 0.0) + jnp.where(where_g == g, early, 0.0), axis=0, keepdims=True
    )

    def at_lane(row, q):
        return jnp.sum(jnp.where(lanes == q, row, 0.0), axis=1, keepdims=True)

    def upright(row):
        return jnp.broadcast_to(row, (128, row.shape[1])).T[:, :1]

    def wanted_of(q):
        count = at_lane(total, q)
        asked = jnp.concatenate([msg[q, 1 + i:2 + i, :] for i in range(K // 128)], axis=1)
        return asked - jnp.floor((asked + 0.5) / count) * count

    span = 2.0 * G * R * S
    key = place
    for q in range(G):
        key = key + jnp.where(labr == q, at_lane(ahead, q) + q * span, 0.0)
    hits = jnp.zeros((8, tok), F32)
    for q in range(G):
        same = jnp.where(upright(wanted_of(q) + q * span) == key, 1.0, 0.0)
        hits = hits + jnp.sum(same.reshape(K // 8, 8, tok), axis=0)
    hit = (jnp.sum(hits, axis=0, keepdims=True) > 0.0) & (place >= A)
    seeds = jnp.where(hit, mem, 0.0)
    seed_place, seed_count = before(seeds)
    seeds_all = jnp.sum(seed_count * mem, axis=0, keepdims=True)
    place = jnp.where(
        place < A, place, jnp.where(hit, seed_place + A, place + seeds_all - seed_place)
    )
    chosen = chosen_of(place.astype(jnp.int32))
    for j in range(1, per):
        send_piece(j, chosen[:G - 1])
    for i in range(S // T):
        inc[g, pl.ds(i * T, T), :] = moved(chosen[G - 1:], i * T, T)

    slot_of = labr.astype(F32) * S + place
    for b in range(tok // 128):
        wide = jnp.broadcast_to(slot_of[:, b * 128:(b + 1) * 128], (128, 128))
        target[pl.ds(b * 128, 128), :] = wide.T[:, :1].astype(jnp.int32)

    mine = jnp.where(lax.broadcasted_iota(jnp.int32, (GP, 128), 1) == g, 1.0, 0.0)
    totals_g = jnp.sum(totals * mine, axis=1, keepdims=True)
    early_g = jnp.sum(early * mine, axis=1, keepdims=True)
    here_g = jnp.sum(tab[r] * mine, axis=1, keepdims=True)
    n_here = [here_g[q:q + 1] for q in range(G)]
    wide_w = wanted_of(g)
    tall_w = upright(wide_w)
    before_k = lax.broadcasted_iota(jnp.int32, (K, K), 0) < lax.broadcasted_iota(jnp.int32, (K, K), 1)
    again = jnp.max(jnp.where((tall_w == wide_w) & before_k, 1.0, 0.0), axis=0, keepdims=True)
    lower = jnp.sum(jnp.where(wide_w < tall_w, 1.0 - again, 0.0), axis=1, keepdims=True)
    slots = lax.broadcasted_iota(jnp.int32, (1, F), 1).astype(F32)
    base = jnp.zeros((1, 1), F32)
    for q in range(G):
        start = base + early_g[q:q + 1]
        base = base + totals_g[q:q + 1]
        local = tall_w - start
        fewer = jnp.sum(jnp.where(wide_w < start + A, 1.0 - again, 0.0), axis=1, keepdims=True)
        slot = jnp.where(local < A, local, lower - fewer + A)
        slot = jnp.where((local >= 0.0) & (local < n_here[q]), slot, -1.0)
        pick = jnp.where(slot == slots, 1.0, 0.0).astype(BF16)
        lhst[0, :, pl.ds(q * S, F)] = pick[:H]
        lhst[1, :, pl.ds(q * S, F)] = pick[H:]

    for j in range(early_pieces):
        wait_piece(j)

    C = E // 2

    def half_sum(h, e):
        rows = inc[:, :, pl.ds(e * C, C)].reshape(N, C)
        return jnp.dot(lhst[h], rows, preferred_element_type=F32)

    def seed_sum(h, e):
        total = None
        for q in range(G):
            part = jnp.dot(
                lhst[h, :, pl.ds(q * S, F)], inc[q, pl.ds(0, F), pl.ds(e * C, C)],
                preferred_element_type=F32,
            )
            total = part if total is None else total + part
        return total

    def big(t, finish, meanwhile=None, half_sum=half_sum):
        slot = t % 2
        first = []
        sends = []
        for e in range(2):
            s1s[e] = half_sum(oc, e).astype(BF16)
            d = copy(s1s.at[e], s1r.at[slot, e], s1_ss.at[slot, e], s1_rs.at[slot, e], (g, partner))
            d.start()
            first.append(d)
        for e in range(2):
            acc[e] = half_sum(c, e)
        for d in first:
            d.wait_recv()
        for m in range(M):
            at = pl.ds(m * Z * QM, Z * QM)
            for e in range(2):
                both = acc[e, at, :] + s1r[slot, e, at, :].astype(F32)
                acc[e, at, :] = both
                s2s[m, :, :, pl.ds(e * C, C)] = both.astype(BF16).reshape(Z, QM, C)
            for off in range(1, Z):
                to = (z + off) % Z
                d = copy(
                    s2s.at[m, to], s2r.at[slot, m, z],
                    s2_ss.at[slot, m, off], s2_rs.at[slot, m, z], (g, to * 2 + c),
                )
                d.start()
                sends.append(d)
        for m in range(M):
            at = pl.ds(pl.multiple_of(m * Z * QM + z * QM, QM), QM)
            own = jnp.concatenate([acc[0, at, :], acc[1, at, :]], axis=1)
            for off in range(1, Z):
                src = (z + off) % Z
                part = s2r.at[slot, m, src]
                copy(
                    part, part, s2_ss.at[slot, m, off], s2_rs.at[slot, m, src], (g, src * 2 + c)
                ).wait_recv()
                own = own + s2r[slot, m, src].astype(F32)
            mine = cent.at[slot, c, m, z]
            cent[slot, c, m, z] = finish(own, m).astype(BF16)
            for off in range(1, Z):
                to = (z + off) % Z
                d = copy(mine, mine, g_ss.at[slot, m, off], g_rs.at[slot, m, z], (g, to * 2 + c))
                d.start()
                sends.append(d)
            d = copy(mine, mine, f_ss.at[slot, m, z], f_rs.at[slot, m, z], (g, partner))
            d.start()
            sends.append(d)
        if meanwhile is not None:
            meanwhile()
        for m in range(M):
            for off in range(1, Z):
                src = (z + off) % Z
                part = cent.at[slot, c, m, src]
                copy(part, part, g_ss.at[slot, m, off], g_rs.at[slot, m, src], (g, src * 2 + c)).wait_recv()
                d = copy(part, part, f_ss.at[slot, m, src], f_rs.at[slot, m, src], (g, partner))
                d.start()
                sends.append(d)
        for m in range(M):
            for off in range(Z):
                src = (z + off) % Z
                part = cent.at[slot, oc, m, src]
                copy(part, part, f_ss.at[slot, m, src], f_rs.at[slot, m, src], (g, partner)).wait_recv()
        for d in first + sends:
            d.wait_send()

    def column_start(t, part8):
        slot = t % 2
        cs[slot, r] = jnp.sum(part8, axis=0, keepdims=True)
        sends = []
        for off in sorted(range(1, R), key=lambda o: -min(o, R - o)):
            to = (r + off) % R
            d = copy(cs.at[slot, r], cs.at[slot, r], cs_ss.at[slot, off], cs_rs.at[slot, r], (g, to))
            d.start()
            sends.append(d)
        return sends

    def column_sum(t, sends):
        slot = t % 2
        for off in range(1, R):
            src = (r + off) % R
            part = cs.at[slot, src]
            copy(part, part, cs_ss.at[slot, off], cs_rs.at[slot, src], (g, src)).wait_recv()
        whole = cs[slot, 0]
        for q in range(1, R):
            whole = whole + cs[slot, q]
        for d in sends:
            d.wait_send()
        return whole

    tiles = N // T
    zero8 = jnp.zeros((8, K), F32)

    def down(v):
        return jnp.sum(v.reshape(v.shape[0] // 8, 8, K), axis=0)

    def assign_rows():
        for off in range(1, G):
            src = (g + off) % G
            part = ret.at[src]
            copy(part, part, r_ss.at[off], r_rs.at[src], (src, r)).wait_recv()

        def one(i, carry):
            at = pl.ds(pl.multiple_of(i * 256, 256), 256)
            hot = jnp.where(
                lax.broadcasted_iota(jnp.int32, (256, N), 1) == target[at, :], 1.0, 0.0
            ).astype(BF16)
            assign_ref[at, :] = jnp.dot(
                hot, ret[...].reshape(N, K), preferred_element_type=F32
            ).astype(BF16)
            return carry

        lax.fori_loop(0, tok // 256, one, 0)

    big(0, lambda v, m: v, None, seed_sum)
    step = 0
    back_sends = []
    for round_index in range(ROUNDS):
        last = round_index == ROUNDS - 1
        slot = round_index % 2
        part = zero8
        areas = [(0, F)] + pieces[early_pieces:] if round_index == 0 else [(0, S)]
        for j, (start, size) in enumerate(areas):
            if round_index == 0 and j > 0:
                wait_piece(early_pieces + j - 1)
            for q in range(G):
                v = lax.dot_general(
                    inc[q, pl.ds(start, size), :], cent[slot].reshape(K, E),
                    (((1,), (1,)), ((), ())), preferred_element_type=F32,
                )
                at = (lax.broadcasted_iota(jnp.int32, (size, 1), 0) + start).astype(F32)
                v = jnp.where(at < n_here[q], jnp.exp(v * 10.0), 0.0)
                plan[pl.ds(q * S + start, size), :] = v
                part = part + down(v)
        for it in range(ITERS):
            col = 1.0 / column_sum(step, column_start(step, part))
            step += 1
            part = zero8
            for i in range(tiles):
                at = pl.ds(i * T, T)
                v = plan[at, :] * col
                s = jnp.sum(v, axis=1, keepdims=True)
                u = jnp.where(s > 0.0, 1.0 / s, 0.0)
                if it < ITERS - 1:
                    part = part + down(plan[at, :] * u)
                else:
                    v = v * u
                    if last:
                        planb[at, :] = v.astype(BF16)
                        part = part + down(v)
                    vt = v.T.astype(BF16)
                    lhst[0, :, at] = vt[:H]
                    lhst[1, :, at] = vt[H:]
        if not last:
            big(
                round_index + 1,
                lambda v, m: v * lax.rsqrt(jnp.sum(v * v, axis=1, keepdims=True) + 1e-06),
            )
        else:
            for off in range(1, G):
                to = (g + off) % G
                d = copy(
                    planb.at[pl.ds(pl.multiple_of(to * S, S), S), :], ret.at[g],
                    r_ss.at[off], r_rs.at[g], (to, r),
                )
                d.start()
                back_sends.append(d)
            ret[g] = planb[pl.ds(pl.multiple_of(g * S, S), S), :]
            weight_sends = column_start(step, part)
            weights = []

            def mean_of(v, m):
                if m == 0:
                    weights.append(column_sum(step, weight_sends))
                wide = lax.broadcasted_iota(jnp.int32, (QM, K), 0) + (c * H + m * Z * QM + z * QM)
                pick = wide == lax.broadcasted_iota(jnp.int32, (QM, K), 1)
                return v / jnp.sum(jnp.where(pick, weights[0], 0.0), axis=1, keepdims=True)

            big(ROUNDS, mean_of, assign_rows)
            means_ref[...] = cent[ROUNDS % 2].reshape(K, E).astype(F32)

    for d in count_sends + row_sends + rank_sends + back_sends:
        d.wait_send()


def on_device(G, R, embeddings, labels, init_idx):
    tok, E = embeddings.shape
    K = init_idx.shape[1]
    S = 2 * tok // G
    T = min(256, S)
    N = G * S
    Z = R // 2
    Q = K // 2 // Z
    M = 2 if Q % 32 == 0 else 1
    QM = Q // M
    A = min(64, S)
    F = min(S, A + K)
    early = [(0, A)] + cut(A, F, 128)
    pieces = early + cut(F, S, 128)
    per = len(pieces)
    dma = pltpu.SemaphoreType.DMA
    vm = pltpu.VMEM
    assign, means = pl.pallas_call(
        functools.partial(kernel, G, R, tok, E, K, S, T, A, pieces, len(early)),
        out_shape=(
            jax.ShapeDtypeStruct((tok, K), BF16),
            jax.ShapeDtypeStruct((K, E), F32),
        ),
        in_specs=[pl.BlockSpec(memory_space=pltpu.HBM)] + [pl.BlockSpec(memory_space=pltpu.VMEM)] * 2,
        out_specs=[pl.BlockSpec(memory_space=pltpu.VMEM)] * 2,
        scratch_shapes=[
            vm((tok, E), BF16),
            vm((tok, E), BF16),
            vm((G - 1, S, E), BF16),
            vm((G, S, E), BF16),
            vm((N, K), F32),
            vm((N, K), BF16),
            vm((2, K // 2, N), BF16),
            vm((2, K // 2, E // 2), F32),
            vm((G, S, K), BF16),
            vm((tok, 1), jnp.int32),
            vm((G, 8, 128), F32),
            vm((R, -(-G // 8) * 8, 128), F32),
            vm((2, R, 1, K), F32),
            vm((2, K // 2, E // 2), BF16),
            vm((2, 2, K // 2, E // 2), BF16),
            vm((M, Z, QM, E), BF16),
            vm((2, M, Z, QM, E), BF16),
            vm((2, 2, M, Z, QM, E), BF16),
            dma((tok // x_sem_rows(tok),)),
            dma((G * per,)), dma((G * per,)),
            dma((G,)), dma((G,)),
            dma((R,)), dma((R,)),
            dma((2, R)), dma((2, R)),
            dma((2, 2)), dma((2, 2)),
            dma((2, M, Z)), dma((2, M, Z)),
            dma((2, M, Z)), dma((2, M, Z)),
            dma((2, M, Z)), dma((2, M, Z)),
            dma((G,)), dma((G,)),
        ],
        compiler_params=pltpu.CompilerParams(
            collective_id=0, has_side_effects=True, vmem_limit_bytes=48 * 1024 * 1024,
        ),
    )(embeddings, labels.reshape(1, tok), init_idx)
    return (assign, means[None])


def solution(mesh):
    return jax.shard_map(
        functools.partial(on_device, mesh.shape["sc"], mesh.shape["rows"]),
        mesh=mesh,
        in_specs=(P(("sc", "rows"), None), P(("sc", "rows"), None), P("sc", None)),
        out_specs=(P(("sc", "rows"), None), P("sc", None, None)),
        check_vma=False,
    )
```

```python
import functools
import math

import jax
import jax.numpy as jnp
from jax import lax
from jax.experimental import pallas as pl
from jax.experimental.pallas import tpu as pltpu
from jax.sharding import PartitionSpec as P

ITERS = 3
ROUNDS = 3
MESH = pl.DeviceIdType.MESH
F32 = jnp.float32
BF16 = jnp.bfloat16


def x_sem_rows(tok):
    return min(256, tok)


def cut(first, last, size):
    return [(at, min(size, last - at)) for at in range(first, last, size)]


def kernel(
    G, R, tok, E, K, S, T, A, pieces, early_pieces,
    x_ref, labr_hbm, init_hbm,
    assign_ref, means_ref,
    labr_ref, init_ref, xin, xu, out, inc, plan, planb, lhst, acc, ret, target,
    msg, tab, cs, s1s, s1r, s2s, s2r, cent,
    x_sem, l_sem, i_sem, d_ss, d_rs, c_ss, c_rs, k_ss, k_rs, cs_ss, cs_rs,
    s1_ss, s1_rs, s2_ss, s2_rs, g_ss, g_rs, f_ss, f_rs, r_ss, r_rs,
):
    g = lax.axis_index("sc")
    r = lax.axis_index("rows")
    Z = R // 2
    H = K // 2
    Q = H // Z
    M = 2 if Q % 32 == 0 else 1
    QM = Q // M
    N = G * S
    GP = -(-G // 8) * 8
    F = pieces[early_pieces - 1][0] + pieces[early_pieces - 1][1]
    per = len(pieces)
    XT = x_sem_rows(tok)
    z = r // 2
    c = r % 2
    oc = 1 - c
    partner = z * 2 + oc

    def copy(src, dst, ss, rs, to):
        return pltpu.make_async_remote_copy(
            src_ref=src, dst_ref=dst, send_sem=ss, recv_sem=rs,
            device_id=to, device_id_type=MESH,
        )

    barrier = pltpu.get_barrier_semaphore()
    for off in range(1, R):
        pl.semaphore_signal(barrier, inc=1, device_id=(g, (r + off) % R), device_id_type=MESH)
    for off in range(1, G):
        pl.semaphore_signal(barrier, inc=1, device_id=((g + off) % G, r), device_id_type=MESH)

    small = [
        pltpu.make_async_copy(labr_hbm, labr_ref, l_sem),
        pltpu.make_async_copy(init_hbm, init_ref, i_sem),
    ]
    for d in small:
        d.start()
    for i in range(tok // XT):
        at = pl.ds(i * XT, XT)
        pltpu.make_async_copy(x_ref.at[at, :], xin.at[at, :], x_sem.at[i]).start()
    for d in small:
        d.wait()

    lanes = lax.broadcasted_iota(jnp.int32, (1, 128), 1)
    sub = lax.broadcasted_iota(jnp.int32, (128, 128), 0)
    lane = lax.broadcasted_iota(jnp.int32, (128, 128), 1)
    tri = jnp.where(sub < lane, 1.0, 0.0).astype(BF16)
    labr = labr_ref[...]
    mem = jnp.where(lax.broadcasted_iota(jnp.int32, (16, tok), 0) == labr, 1.0, 0.0)

    def before(marks):
        seen = jnp.zeros((16, 1), F32)
        places = []
        for b in range(tok // 128):
            part = marks[:, b * 128:(b + 1) * 128]
            ahead = jnp.dot(part.astype(BF16), tri, preferred_element_type=F32) + seen
            places.append(jnp.sum(ahead * mem[:, b * 128:(b + 1) * 128], axis=0, keepdims=True))
            seen = seen + jnp.sum(part, axis=1, keepdims=True)
        return jnp.concatenate(places, axis=1), seen

    place, held = before(mem)
    msg[g] = jnp.zeros((8, 128), F32)
    msg[g, 0:1, :] = jnp.sum(jnp.where(sub[:16] == lane[:16], held, 0.0), axis=0, keepdims=True)
    for i in range(K // 128):
        msg[g, 1 + i:2 + i, :] = init_ref[:, i * 128:(i + 1) * 128].astype(F32)

    pl.semaphore_wait(barrier, R - 1 + G - 1)

    count_sends = []
    for off in range(1, G):
        d = copy(msg.at[g], msg.at[g], c_ss.at[off], c_rs.at[g], ((g + off) % G, r))
        d.start()
        count_sends.append(d)

    for i in range(tok // XT):
        at = pl.ds(i * XT, XT)
        pltpu.make_async_copy(x_ref.at[at, :], xin.at[at, :], x_sem.at[i]).wait()
        v = xin[at, :].astype(F32)
        scale = lax.rsqrt(jnp.mean(v * v, axis=1, keepdims=True) + 1e-05) * (1.0 / math.sqrt(E))
        xu[at, :] = (v * scale).astype(BF16)

    row_sends = []

    def moved(chosen, start, size):
        slot = lax.broadcasted_iota(jnp.int32, (size, tok), 0) + start
        perm = jnp.concatenate([jnp.where(slot == one, 1.0, 0.0).astype(BF16) for one in chosen], axis=0)
        return jnp.dot(perm, xu[...], preferred_element_type=F32).astype(BF16)

    def send_piece(j, chosen):
        start, size = pieces[j]
        at = pl.ds(start, size)
        block = moved(chosen, start, size)
        for off in range(1, G):
            out[off - 1, at, :] = block[(off - 1) * size:off * size]
            d = copy(
                out.at[off - 1, at, :], inc.at[g, at, :],
                d_ss.at[off * per + j], d_rs.at[g * per + j], ((g + off) % G, r),
            )
            d.start()
            row_sends.append(d)

    def wait_piece(j):
        for off in range(1, G):
            src = (g + off) % G
            part = inc.at[src, pl.ds(*pieces[j]), :]
            copy(part, part, d_ss.at[off * per + j], d_rs.at[src * per + j], (src, r)).wait_recv()

    def chosen_of(place_i):
        return [jnp.where(labr == (g + off) % G, place_i, -1) for off in range(1, G + 1)]

    send_piece(0, chosen_of(place.astype(jnp.int32))[:G - 1])

    for off in range(1, G):
        src = (g + off) % G
        copy(msg.at[src], msg.at[src], c_ss.at[off], c_rs.at[src], (src, r)).wait_recv()
    tab[r] = jnp.zeros((GP, 128), F32)
    for q in range(G):
        tab[r, q:q + 1, :] = msg[q, 0:1, :]
    rank_sends = []
    for off in range(1, R):
        to = (r + off) % R
        d = copy(tab.at[r], tab.at[r], k_ss.at[off], k_rs.at[r], (g, to))
        d.start()
        rank_sends.append(d)
    for off in range(1, R):
        src = (r + off) % R
        copy(tab.at[src], tab.at[src], k_ss.at[off], k_rs.at[src], (g, src)).wait_recv()
    totals = jnp.zeros((GP, 128), F32)
    early = jnp.zeros((GP, 128), F32)
    for q in range(R):
        rows = tab[q]
        totals = totals + rows
        early = early + jnp.where(r > q, rows, 0.0)
    total = jnp.sum(totals, axis=0, keepdims=True)
    where_g = lax.broadcasted_iota(jnp.int32, (GP, 128), 0)
    ahead = jnp.sum(
        jnp.where(where_g < g, totals, 0.0) + jnp.where(where_g == g, early, 0.0), axis=0, keepdims=True
    )

    def at_lane(row, q):
        return jnp.sum(jnp.where(lanes == q, row, 0.0), axis=1, keepdims=True)

    def upright(row):
        return jnp.broadcast_to(row, (128, row.shape[1])).T[:, :1]

    def wanted_of(q):
        count = at_lane(total, q)
        asked = jnp.concatenate([msg[q, 1 + i:2 + i, :] for i in range(K // 128)], axis=1)
        return asked - jnp.floor((asked + 0.5) / count) * count

    span = 2.0 * G * R * S
    key = place
    for q in range(G):
        key = key + jnp.where(labr == q, at_lane(ahead, q) + q * span, 0.0)
    hits = jnp.zeros((8, tok), F32)
    for q in range(G):
        same = jnp.where(upright(wanted_of(q) + q * span) == key, 1.0, 0.0)
        hits = hits + jnp.sum(same.reshape(K // 8, 8, tok), axis=0)
    hit = (jnp.sum(hits, axis=0, keepdims=True) > 0.0) & (place >= A)
    seeds = jnp.where(hit, mem, 0.0)
    seed_place, seed_count = before(seeds)
    seeds_all = jnp.sum(seed_count * mem, axis=0, keepdims=True)
    place = jnp.where(
        place < A, place, jnp.where(hit, seed_place + A, place + seeds_all - seed_place)
    )
    chosen = chosen_of(place.astype(jnp.int32))
    for j in range(1, per):
        send_piece(j, chosen[:G - 1])
    for i in range(S // T):
        inc[g, pl.ds(i * T, T), :] = moved(chosen[G - 1:], i * T, T)

    slot_of = labr.astype(F32) * S + place
    for b in range(tok // 128):
        wide = jnp.broadcast_to(slot_of[:, b * 128:(b + 1) * 128], (128, 128))
        target[pl.ds(b * 128, 128), :] = wide.T[:, :1].astype(jnp.int32)

    mine = jnp.where(lax.broadcasted_iota(jnp.int32, (GP, 128), 1) == g, 1.0, 0.0)
    totals_g = jnp.sum(totals * mine, axis=1, keepdims=True)
    early_g = jnp.sum(early * mine, axis=1, keepdims=True)
    here_g = jnp.sum(tab[r] * mine, axis=1, keepdims=True)
    n_here = [here_g[q:q + 1] for q in range(G)]
    wide_w = wanted_of(g)
    tall_w = upright(wide_w)
    before_k = lax.broadcasted_iota(jnp.int32, (K, K), 0) < lax.broadcasted_iota(jnp.int32, (K, K), 1)
    again = jnp.max(jnp.where((tall_w == wide_w) & before_k, 1.0, 0.0), axis=0, keepdims=True)
    lower = jnp.sum(jnp.where(wide_w < tall_w, 1.0 - again, 0.0), axis=1, keepdims=True)
    slots = lax.broadcasted_iota(jnp.int32, (1, F), 1).astype(F32)
    base = jnp.zeros((1, 1), F32)
    for q in range(G):
        start = base + early_g[q:q + 1]
        base = base + totals_g[q:q + 1]
        local = tall_w - start
        fewer = jnp.sum(jnp.where(wide_w < start + A, 1.0 - again, 0.0), axis=1, keepdims=True)
        slot = jnp.where(local < A, local, lower - fewer + A)
        slot = jnp.where((local >= 0.0) & (local < n_here[q]), slot, -1.0)
        pick = jnp.where(slot == slots, 1.0, 0.0).astype(BF16)
        lhst[0, :, pl.ds(q * S, F)] = pick[:H]
        lhst[1, :, pl.ds(q * S, F)] = pick[H:]

    for j in range(early_pieces):
        wait_piece(j)

    C = E // 2

    def half_sum(h, e):
        rows = inc[:, :, pl.ds(e * C, C)].reshape(N, C)
        return jnp.dot(lhst[h], rows, preferred_element_type=F32)

    def seed_sum(h, e):
        total = None
        for q in range(G):
            part = jnp.dot(
                lhst[h, :, pl.ds(q * S, F)], inc[q, pl.ds(0, F), pl.ds(e * C, C)],
                preferred_element_type=F32,
            )
            total = part if total is None else total + part
        return total

    def big(t, finish, meanwhile=None, half_sum=half_sum):
        slot = t % 2
        first = []
        sends = []
        for e in range(2):
            s1s[e] = half_sum(oc, e).astype(BF16)
            d = copy(s1s.at[e], s1r.at[slot, e], s1_ss.at[slot, e], s1_rs.at[slot, e], (g, partner))
            d.start()
            first.append(d)
        for e in range(2):
            acc[e] = half_sum(c, e)
        for d in first:
            d.wait_recv()
        for m in range(M):
            at = pl.ds(m * Z * QM, Z * QM)
            for e in range(2):
                both = acc[e, at, :] + s1r[slot, e, at, :].astype(F32)
                acc[e, at, :] = both
                s2s[m, :, :, pl.ds(e * C, C)] = both.astype(BF16).reshape(Z, QM, C)
            for off in range(1, Z):
                to = (z + off) % Z
                d = copy(
                    s2s.at[m, to], s2r.at[slot, m, z],
                    s2_ss.at[slot, m, off], s2_rs.at[slot, m, z], (g, to * 2 + c),
                )
                d.start()
                sends.append(d)
        for m in range(M):
            at = pl.ds(pl.multiple_of(m * Z * QM + z * QM, QM), QM)
            own = jnp.concatenate([acc[0, at, :], acc[1, at, :]], axis=1)
            for off in range(1, Z):
                src = (z + off) % Z
                part = s2r.at[slot, m, src]
                copy(
                    part, part, s2_ss.at[slot, m, off], s2_rs.at[slot, m, src], (g, src * 2 + c)
                ).wait_recv()
                own = own + s2r[slot, m, src].astype(F32)
            mine = cent.at[slot, c, m, z]
            cent[slot, c, m, z] = finish(own, m).astype(BF16)
            for off in range(1, Z):
                to = (z + off) % Z
                d = copy(mine, mine, g_ss.at[slot, m, off], g_rs.at[slot, m, z], (g, to * 2 + c))
                d.start()
                sends.append(d)
            d = copy(mine, mine, f_ss.at[slot, m, z], f_rs.at[slot, m, z], (g, partner))
            d.start()
            sends.append(d)
        if meanwhile is not None:
            meanwhile()
        for m in range(M):
            for off in range(1, Z):
                src = (z + off) % Z
                part = cent.at[slot, c, m, src]
                copy(part, part, g_ss.at[slot, m, off], g_rs.at[slot, m, src], (g, src * 2 + c)).wait_recv()
                d = copy(part, part, f_ss.at[slot, m, src], f_rs.at[slot, m, src], (g, partner))
                d.start()
                sends.append(d)
        for m in range(M):
            for off in range(Z):
                src = (z + off) % Z
                part = cent.at[slot, oc, m, src]
                copy(part, part, f_ss.at[slot, m, src], f_rs.at[slot, m, src], (g, partner)).wait_recv()
        for d in first + sends:
            d.wait_send()

    def column_start(t, part8):
        slot = t % 2
        cs[slot, r] = jnp.sum(part8, axis=0, keepdims=True)
        sends = []
        for off in sorted(range(1, R), key=lambda o: -min(o, R - o)):
            to = (r + off) % R
            d = copy(cs.at[slot, r], cs.at[slot, r], cs_ss.at[slot, off], cs_rs.at[slot, r], (g, to))
            d.start()
            sends.append(d)
        return sends

    def column_sum(t, sends):
        slot = t % 2
        for off in range(1, R):
            src = (r + off) % R
            part = cs.at[slot, src]
            copy(part, part, cs_ss.at[slot, off], cs_rs.at[slot, src], (g, src)).wait_recv()
        whole = cs[slot, 0]
        for q in range(1, R):
            whole = whole + cs[slot, q]
        for d in sends:
            d.wait_send()
        return whole

    tiles = N // T
    zero8 = jnp.zeros((8, K), F32)

    def down(v):
        return jnp.sum(v.reshape(v.shape[0] // 8, 8, K), axis=0)

    def assign_rows():
        for off in range(1, G):
            src = (g + off) % G
            part = ret.at[src]
            copy(part, part, r_ss.at[off], r_rs.at[src], (src, r)).wait_recv()

        def one(i, carry):
            at = pl.ds(pl.multiple_of(i * 256, 256), 256)
            hot = jnp.where(
                lax.broadcasted_iota(jnp.int32, (256, N), 1) == target[at, :], 1.0, 0.0
            ).astype(BF16)
            assign_ref[at, :] = jnp.dot(
                hot, ret[...].reshape(N, K), preferred_element_type=F32
            ).astype(BF16)
            return carry

        lax.fori_loop(0, tok // 256, one, 0)

    big(0, lambda v, m: v, None, seed_sum)
    step = 0
    back_sends = []
    for round_index in range(ROUNDS):
        last = round_index == ROUNDS - 1
        slot = round_index % 2
        part = zero8
        areas = [(0, F)] + pieces[early_pieces:] if round_index == 0 else [(0, S)]
        for j, (start, size) in enumerate(areas):
            if round_index == 0 and j > 0:
                wait_piece(early_pieces + j - 1)
            for q in range(G):
                v = lax.dot_general(
                    inc[q, pl.ds(start, size), :], cent[slot].reshape(K, E),
                    (((1,), (1,)), ((), ())), preferred_element_type=F32,
                )
                at = (lax.broadcasted_iota(jnp.int32, (size, 1), 0) + start).astype(F32)
                v = jnp.where(at < n_here[q], jnp.exp(v * 10.0), 0.0)
                plan[pl.ds(q * S + start, size), :] = v
                part = part + down(v)
        for it in range(ITERS):
            col = 1.0 / column_sum(step, column_start(step, part))
            step += 1
            part = zero8
            for i in range(tiles):
                at = pl.ds(i * T, T)
                v = plan[at, :] * col
                s = jnp.sum(v, axis=1, keepdims=True)
                u = jnp.where(s > 0.0, 1.0 / s, 0.0)
                if it < ITERS - 1:
                    part = part + down(plan[at, :] * u)
                else:
                    v = v * u
                    if last:
                        planb[at, :] = v.astype(BF16)
                        part = part + down(v)
                    vt = v.T.astype(BF16)
                    lhst[0, :, at] = vt[:H]
                    lhst[1, :, at] = vt[H:]
        if not last:
            big(
                round_index + 1,
                lambda v, m: v * lax.rsqrt(jnp.sum(v * v, axis=1, keepdims=True) + 1e-06),
            )
        else:
            for off in range(1, G):
                to = (g + off) % G
                d = copy(
                    planb.at[pl.ds(pl.multiple_of(to * S, S), S), :], ret.at[g],
                    r_ss.at[off], r_rs.at[g], (to, r),
                )
                d.start()
                back_sends.append(d)
            ret[g] = planb[pl.ds(pl.multiple_of(g * S, S), S), :]
            weight_sends = column_start(step, part)
            weights = []

            def mean_of(v, m):
                if m == 0:
                    weights.append(column_sum(step, weight_sends))
                wide = lax.broadcasted_iota(jnp.int32, (QM, K), 0) + (c * H + m * Z * QM + z * QM)
                pick = wide == lax.broadcasted_iota(jnp.int32, (QM, K), 1)
                return v / jnp.sum(jnp.where(pick, weights[0], 0.0), axis=1, keepdims=True)

            big(ROUNDS, mean_of, assign_rows)
            means_ref[...] = cent[ROUNDS % 2].reshape(K, E).astype(F32)

    for d in count_sends + row_sends + rank_sends + back_sends:
        d.wait_send()


def on_device(G, R, embeddings, labels, init_idx):
    tok, E = embeddings.shape
    K = init_idx.shape[1]
    S = 2 * tok // G
    T = min(256, S)
    N = G * S
    Z = R // 2
    Q = K // 2 // Z
    M = 2 if Q % 32 == 0 else 1
    QM = Q // M
    A = min(64, S)
    F = min(S, A + K)
    early = [(0, A)] + cut(A, F, 128)
    pieces = early + cut(F, S, 128)
    per = len(pieces)
    dma = pltpu.SemaphoreType.DMA
    vm = pltpu.VMEM
    assign, means = pl.pallas_call(
        functools.partial(kernel, G, R, tok, E, K, S, T, A, pieces, len(early)),
        out_shape=(
            jax.ShapeDtypeStruct((tok, K), BF16),
            jax.ShapeDtypeStruct((K, E), F32),
        ),
        in_specs=[pl.BlockSpec(memory_space=pltpu.HBM)] * 3,
        out_specs=[pl.BlockSpec(memory_space=pltpu.VMEM)] * 2,
        scratch_shapes=[
            vm((1, tok), jnp.int32),
            vm((1, K), jnp.int32),
            vm((tok, E), BF16),
            vm((tok, E), BF16),
            vm((G - 1, S, E), BF16),
            vm((G, S, E), BF16),
            vm((N, K), F32),
            vm((N, K), BF16),
            vm((2, K // 2, N), BF16),
            vm((2, K // 2, E // 2), F32),
            vm((G, S, K), BF16),
            vm((tok, 1), jnp.int32),
            vm((G, 8, 128), F32),
            vm((R, -(-G // 8) * 8, 128), F32),
            vm((2, R, 1, K), F32),
            vm((2, K // 2, E // 2), BF16),
            vm((2, 2, K // 2, E // 2), BF16),
            vm((M, Z, QM, E), BF16),
            vm((2, M, Z, QM, E), BF16),
            vm((2, 2, M, Z, QM, E), BF16),
            dma((tok // x_sem_rows(tok),)), dma, dma,
            dma((G * per,)), dma((G * per,)),
            dma((G,)), dma((G,)),
            dma((R,)), dma((R,)),
            dma((2, R)), dma((2, R)),
            dma((2, 2)), dma((2, 2)),
            dma((2, M, Z)), dma((2, M, Z)),
            dma((2, M, Z)), dma((2, M, Z)),
            dma((2, M, Z)), dma((2, M, Z)),
            dma((G,)), dma((G,)),
        ],
        compiler_params=pltpu.CompilerParams(
            collective_id=0, has_side_effects=True, vmem_limit_bytes=48 * 1024 * 1024,
        ),
    )(*[pltpu.with_memory_space_constraint(v, pltpu.HBM) for v in (embeddings, labels.reshape(1, tok), init_idx)])
    return (assign, means[None])


def solution(mesh):
    return jax.shard_map(
        functools.partial(on_device, mesh.shape["sc"], mesh.shape["rows"]),
        mesh=mesh,
        in_specs=(P(("sc", "rows"), None), P(("sc", "rows"), None), P("sc", None)),
        out_specs=(P(("sc", "rows"), None), P("sc", None, None)),
        check_vma=False,
    )
```

```python
import functools
import math

import jax
import jax.numpy as jnp
from jax import lax
from jax.experimental import pallas as pl
from jax.experimental.pallas import tpu as pltpu
from jax.sharding import PartitionSpec as P

ITERS = 3
ROUNDS = 3
MESH = pl.DeviceIdType.MESH
F32 = jnp.float32
BF16 = jnp.bfloat16


def x_sem_rows(tok):
    return min(256, tok)


def cut(first, last, size):
    return [(at, min(size, last - at)) for at in range(first, last, size)]


def kernel(
    G, R, tok, E, K, S, T, A, pieces, early_pieces,
    x_ref, labr_hbm, init_hbm,
    assign_ref, means_ref,
    labr_ref, init_ref, xin, xu, out, inc, plan, planb, lhst, acc, ret, target,
    msg, tab, cs, s1s, s1r, s2s, s2r, cent,
    x_sem, l_sem, i_sem, d_ss, d_rs, c_ss, c_rs, k_ss, k_rs, cs_ss, cs_rs,
    s1_ss, s1_rs, s2_ss, s2_rs, g_ss, g_rs, f_ss, f_rs, r_ss, r_rs,
):
    g = lax.axis_index("sc")
    r = lax.axis_index("rows")
    Z = R // 2
    H = K // 2
    Q = H // Z
    M = 2 if Q % 32 == 0 else 1
    QM = Q // M
    N = G * S
    GP = -(-G // 8) * 8
    F = pieces[early_pieces - 1][0] + pieces[early_pieces - 1][1]
    per = len(pieces)
    XT = x_sem_rows(tok)
    z = r // 2
    c = r % 2
    oc = 1 - c
    partner = z * 2 + oc

    def copy(src, dst, ss, rs, to):
        return pltpu.make_async_remote_copy(
            src_ref=src, dst_ref=dst, send_sem=ss, recv_sem=rs,
            device_id=to, device_id_type=MESH,
        )

    barrier = pltpu.get_barrier_semaphore()
    for off in range(1, R):
        pl.semaphore_signal(barrier, inc=1, device_id=(g, (r + off) % R), device_id_type=MESH)
    for off in range(1, G):
        pl.semaphore_signal(barrier, inc=1, device_id=((g + off) % G, r), device_id_type=MESH)

    small = [
        pltpu.make_async_copy(labr_hbm, labr_ref, l_sem),
        pltpu.make_async_copy(init_hbm, init_ref, i_sem),
    ]
    for d in small:
        d.start()
    for i in range(tok // XT):
        at = pl.ds(i * XT, XT)
        pltpu.make_async_copy(x_ref.at[at, :], xin.at[at, :], x_sem.at[i]).start()
    for d in small:
        d.wait()

    lanes = lax.broadcasted_iota(jnp.int32, (1, 128), 1)
    sub = lax.broadcasted_iota(jnp.int32, (128, 128), 0)
    lane = lax.broadcasted_iota(jnp.int32, (128, 128), 1)
    tri = jnp.where(sub < lane, 1.0, 0.0).astype(BF16)
    labr = labr_ref[...]
    mem = jnp.where(lax.broadcasted_iota(jnp.int32, (16, tok), 0) == labr, 1.0, 0.0)

    def before(marks):
        seen = jnp.zeros((16, 1), F32)
        places = []
        for b in range(tok // 128):
            part = marks[:, b * 128:(b + 1) * 128]
            ahead = jnp.dot(part.astype(BF16), tri, preferred_element_type=F32) + seen
            places.append(jnp.sum(ahead * mem[:, b * 128:(b + 1) * 128], axis=0, keepdims=True))
            seen = seen + jnp.sum(part, axis=1, keepdims=True)
        return jnp.concatenate(places, axis=1), seen

    place, held = before(mem)
    msg[g] = jnp.zeros((8, 128), F32)
    msg[g, 0:1, :] = jnp.sum(jnp.where(sub[:16] == lane[:16], held, 0.0), axis=0, keepdims=True)
    for i in range(K // 128):
        msg[g, 1 + i:2 + i, :] = init_ref[:, i * 128:(i + 1) * 128].astype(F32)

    pl.semaphore_wait(barrier, R - 1 + G - 1)

    count_sends = []
    for off in range(1, G):
        d = copy(msg.at[g], msg.at[g], c_ss.at[off], c_rs.at[g], ((g + off) % G, r))
        d.start()
        count_sends.append(d)

    for i in range(tok // XT):
        at = pl.ds(i * XT, XT)
        pltpu.make_async_copy(x_ref.at[at, :], xin.at[at, :], x_sem.at[i]).wait()
        v = xin[at, :].astype(F32)
        scale = lax.rsqrt(jnp.mean(v * v, axis=1, keepdims=True) + 1e-05) * (1.0 / math.sqrt(E))
        xu[at, :] = (v * scale).astype(BF16)

    row_sends = []

    def moved(chosen, start, size):
        slot = lax.broadcasted_iota(jnp.int32, (size, tok), 0) + start
        perm = jnp.concatenate([jnp.where(slot == one, 1.0, 0.0).astype(BF16) for one in chosen], axis=0)
        return jnp.dot(perm, xu[...], preferred_element_type=F32).astype(BF16)

    def send_piece(j, chosen):
        start, size = pieces[j]
        at = pl.ds(start, size)
        block = moved(chosen, start, size)
        for off in range(1, G):
            out[off - 1, at, :] = block[(off - 1) * size:off * size]
            d = copy(
                out.at[off - 1, at, :], inc.at[g, at, :],
                d_ss.at[off * per + j], d_rs.at[g * per + j], ((g + off) % G, r),
            )
            d.start()
            row_sends.append(d)

    def wait_piece(j):
        for off in range(1, G):
            src = (g + off) % G
            part = inc.at[src, pl.ds(*pieces[j]), :]
            copy(part, part, d_ss.at[off * per + j], d_rs.at[src * per + j], (src, r)).wait_recv()

    def chosen_of(place_i):
        return [jnp.where(labr == (g + off) % G, place_i, -1) for off in range(1, G + 1)]

    send_piece(0, chosen_of(place.astype(jnp.int32))[:G - 1])

    for off in range(1, G):
        src = (g + off) % G
        copy(msg.at[src], msg.at[src], c_ss.at[off], c_rs.at[src], (src, r)).wait_recv()
    tab[r] = jnp.zeros((GP, 128), F32)
    for q in range(G):
        tab[r, q:q + 1, :] = msg[q, 0:1, :]
    rank_sends = []
    for off in range(1, R):
        to = (r + off) % R
        d = copy(tab.at[r], tab.at[r], k_ss.at[off], k_rs.at[r], (g, to))
        d.start()
        rank_sends.append(d)
    for off in range(1, R):
        src = (r + off) % R
        copy(tab.at[src], tab.at[src], k_ss.at[off], k_rs.at[src], (g, src)).wait_recv()
    totals = jnp.zeros((GP, 128), F32)
    early = jnp.zeros((GP, 128), F32)
    for q in range(R):
        rows = tab[q]
        totals = totals + rows
        early = early + jnp.where(r > q, rows, 0.0)
    total = jnp.sum(totals, axis=0, keepdims=True)
    where_g = lax.broadcasted_iota(jnp.int32, (GP, 128), 0)
    ahead = jnp.sum(
        jnp.where(where_g < g, totals, 0.0) + jnp.where(where_g == g, early, 0.0), axis=0, keepdims=True
    )

    def at_lane(row, q):
        return jnp.sum(jnp.where(lanes == q, row, 0.0), axis=1, keepdims=True)

    def upright(row):
        return jnp.broadcast_to(row, (128, row.shape[1])).T[:, :1]

    def wanted_of(q):
        count = at_lane(total, q)
        asked = jnp.concatenate([msg[q, 1 + i:2 + i, :] for i in range(K // 128)], axis=1)
        return asked - jnp.floor((asked + 0.5) / count) * count

    span = 2.0 * G * R * S
    key = place
    for q in range(G):
        key = key + jnp.where(labr == q, at_lane(ahead, q) + q * span, 0.0)
    hits = jnp.zeros((8, tok), F32)
    for q in range(G):
        same = jnp.where(upright(wanted_of(q) + q * span) == key, 1.0, 0.0)
        hits = hits + jnp.sum(same.reshape(K // 8, 8, tok), axis=0)
    hit = (jnp.sum(hits, axis=0, keepdims=True) > 0.0) & (place >= A)
    seeds = jnp.where(hit, mem, 0.0)
    seed_place, seed_count = before(seeds)
    seeds_all = jnp.sum(seed_count * mem, axis=0, keepdims=True)
    place = jnp.where(
        place < A, place, jnp.where(hit, seed_place + A, place + seeds_all - seed_place)
    )
    chosen = chosen_of(place.astype(jnp.int32))
    for j in range(1, per):
        send_piece(j, chosen[:G - 1])
    for i in range(S // T):
        inc[g, pl.ds(i * T, T), :] = moved(chosen[G - 1:], i * T, T)

    slot_of = labr.astype(F32) * S + place
    for b in range(tok // 128):
        wide = jnp.broadcast_to(slot_of[:, b * 128:(b + 1) * 128], (128, 128))
        target[pl.ds(b * 128, 128), :] = wide.T[:, :1].astype(jnp.int32)

    mine = jnp.where(lax.broadcasted_iota(jnp.int32, (GP, 128), 1) == g, 1.0, 0.0)
    totals_g = jnp.sum(totals * mine, axis=1, keepdims=True)
    early_g = jnp.sum(early * mine, axis=1, keepdims=True)
    here_g = jnp.sum(tab[r] * mine, axis=1, keepdims=True)
    n_here = [here_g[q:q + 1] for q in range(G)]
    wide_w = wanted_of(g)
    tall_w = upright(wide_w)
    before_k = lax.broadcasted_iota(jnp.int32, (K, K), 0) < lax.broadcasted_iota(jnp.int32, (K, K), 1)
    again = jnp.max(jnp.where((tall_w == wide_w) & before_k, 1.0, 0.0), axis=0, keepdims=True)
    lower = jnp.sum(jnp.where(wide_w < tall_w, 1.0 - again, 0.0), axis=1, keepdims=True)
    slots = lax.broadcasted_iota(jnp.int32, (1, F), 1).astype(F32)
    base = jnp.zeros((1, 1), F32)
    for q in range(G):
        start = base + early_g[q:q + 1]
        base = base + totals_g[q:q + 1]
        local = tall_w - start
        fewer = jnp.sum(jnp.where(wide_w < start + A, 1.0 - again, 0.0), axis=1, keepdims=True)
        slot = jnp.where(local < A, local, lower - fewer + A)
        slot = jnp.where((local >= 0.0) & (local < n_here[q]), slot, -1.0)
        pick = jnp.where(slot == slots, 1.0, 0.0).astype(BF16)
        lhst[0, :, pl.ds(q * S, F)] = pick[:H]
        lhst[1, :, pl.ds(q * S, F)] = pick[H:]

    for j in range(early_pieces):
        wait_piece(j)

    C = E // 2

    def half_sum(h, e):
        rows = inc[:, :, pl.ds(e * C, C)].reshape(N, C)
        return jnp.dot(lhst[h], rows, preferred_element_type=F32)

    def seed_sum(h, e):
        total = None
        for q in range(G):
            part = jnp.dot(
                lhst[h, :, pl.ds(q * S, F)], inc[q, pl.ds(0, F), pl.ds(e * C, C)],
                preferred_element_type=F32,
            )
            total = part if total is None else total + part
        return total

    def big(t, finish, theirs, meanwhile=None, half_sum=half_sum):
        slot = t % 2
        first = []
        sends = []
        for m in range(M):
            for e in range(2):
                s1s[m, :, pl.ds(e * C, C)] = theirs[e][m * Z * QM:(m + 1) * Z * QM].astype(BF16)
            d = copy(s1s.at[m], s1r.at[slot, m], s1_ss.at[slot, m], s1_rs.at[slot, m], (g, partner))
            d.start()
            first.append(d)
        for e in range(2):
            acc[e] = half_sum(c, e)
        for m in range(M):
            at = pl.ds(m * Z * QM, Z * QM)
            first[m].wait_recv()
            for e in range(2):
                both = acc[e, at, :] + s1r[slot, m, :, pl.ds(e * C, C)].astype(F32)
                acc[e, at, :] = both
                s2s[m, :, :, pl.ds(e * C, C)] = both.astype(BF16).reshape(Z, QM, C)
            for off in range(1, Z):
                to = (z + off) % Z
                d = copy(
                    s2s.at[m, to], s2r.at[slot, m, z],
                    s2_ss.at[slot, m, off], s2_rs.at[slot, m, z], (g, to * 2 + c),
                )
                d.start()
                sends.append(d)
        for m in range(M):
            at = pl.ds(pl.multiple_of(m * Z * QM + z * QM, QM), QM)
            own = jnp.concatenate([acc[0, at, :], acc[1, at, :]], axis=1)
            for off in range(1, Z):
                src = (z + off) % Z
                part = s2r.at[slot, m, src]
                copy(
                    part, part, s2_ss.at[slot, m, off], s2_rs.at[slot, m, src], (g, src * 2 + c)
                ).wait_recv()
                own = own + s2r[slot, m, src].astype(F32)
            mine = cent.at[slot, c, m, z]
            cent[slot, c, m, z] = finish(own, m).astype(BF16)
            for off in range(1, Z):
                to = (z + off) % Z
                d = copy(mine, mine, g_ss.at[slot, m, off], g_rs.at[slot, m, z], (g, to * 2 + c))
                d.start()
                sends.append(d)
            d = copy(mine, mine, f_ss.at[slot, m, z], f_rs.at[slot, m, z], (g, partner))
            d.start()
            sends.append(d)
        if meanwhile is not None:
            meanwhile()
        for m in range(M):
            for off in range(1, Z):
                src = (z + off) % Z
                part = cent.at[slot, c, m, src]
                copy(part, part, g_ss.at[slot, m, off], g_rs.at[slot, m, src], (g, src * 2 + c)).wait_recv()
                d = copy(part, part, f_ss.at[slot, m, src], f_rs.at[slot, m, src], (g, partner))
                d.start()
                sends.append(d)
        for m in range(M):
            for off in range(Z):
                src = (z + off) % Z
                part = cent.at[slot, oc, m, src]
                copy(part, part, f_ss.at[slot, m, src], f_rs.at[slot, m, src], (g, partner)).wait_recv()
        for d in first + sends:
            d.wait_send()

    def column_start(t, part8):
        slot = t % 2
        cs[slot, r] = jnp.sum(part8, axis=0, keepdims=True)
        sends = []
        for off in sorted(range(1, R), key=lambda o: -min(o, R - o)):
            to = (r + off) % R
            d = copy(cs.at[slot, r], cs.at[slot, r], cs_ss.at[slot, off], cs_rs.at[slot, r], (g, to))
            d.start()
            sends.append(d)
        return sends

    def column_sum(t, sends):
        slot = t % 2
        for off in range(1, R):
            src = (r + off) % R
            part = cs.at[slot, src]
            copy(part, part, cs_ss.at[slot, off], cs_rs.at[slot, src], (g, src)).wait_recv()
        whole = cs[slot, 0]
        for q in range(1, R):
            whole = whole + cs[slot, q]
        for d in sends:
            d.wait_send()
        return whole

    tiles = N // T
    zero8 = jnp.zeros((8, K), F32)

    def down(v):
        return jnp.sum(v.reshape(v.shape[0] // 8, 8, K), axis=0)

    def assign_rows():
        for off in range(1, G):
            src = (g + off) % G
            part = ret.at[src]
            copy(part, part, r_ss.at[off], r_rs.at[src], (src, r)).wait_recv()

        def one(i, carry):
            at = pl.ds(pl.multiple_of(i * 256, 256), 256)
            hot = jnp.where(
                lax.broadcasted_iota(jnp.int32, (256, N), 1) == target[at, :], 1.0, 0.0
            ).astype(BF16)
            assign_ref[at, :] = jnp.dot(
                hot, ret[...].reshape(N, K), preferred_element_type=F32
            ).astype(BF16)
            return carry

        lax.fori_loop(0, tok // 256, one, 0)

    big(0, lambda v, m: v, [seed_sum(oc, e) for e in range(2)], None, seed_sum)
    step = 0
    back_sends = []
    for round_index in range(ROUNDS):
        last = round_index == ROUNDS - 1
        slot = round_index % 2
        part = zero8
        areas = [(0, F)] + pieces[early_pieces:] if round_index == 0 else [(0, S)]
        for j, (start, size) in enumerate(areas):
            if round_index == 0 and j > 0:
                wait_piece(early_pieces + j - 1)
            for q in range(G):
                v = lax.dot_general(
                    inc[q, pl.ds(start, size), :], cent[slot].reshape(K, E),
                    (((1,), (1,)), ((), ())), preferred_element_type=F32,
                )
                at = (lax.broadcasted_iota(jnp.int32, (size, 1), 0) + start).astype(F32)
                v = jnp.where(at < n_here[q], jnp.exp(v * 10.0), 0.0)
                plan[pl.ds(q * S + start, size), :] = v
                part = part + down(v)
        for it in range(ITERS):
            col = 1.0 / column_sum(step, column_start(step, part))
            step += 1
            part = zero8
            if it < ITERS - 1:
                for i in range(tiles):
                    v = plan[pl.ds(i * T, T), :]
                    s = jnp.sum(v * col, axis=1, keepdims=True)
                    part = part + down(v * jnp.where(s > 0.0, 1.0 / s, 0.0))
            else:
                theirs = [None, None]
                for q in range(G):
                    at = pl.ds(q * S, S)
                    v = plan[at, :] * col
                    s = jnp.sum(v, axis=1, keepdims=True)
                    v = v * jnp.where(s > 0.0, 1.0 / s, 0.0)
                    if last:
                        planb[at, :] = v.astype(BF16)
                        part = part + down(v)
                    vt = v.T.astype(BF16)
                    lhst[0, :, at] = vt[:H]
                    lhst[1, :, at] = vt[H:]
                    vo = jnp.where(c == 0, vt[H:], vt[:H])
                    for e in range(2):
                        d = jnp.dot(vo, inc[q, :, pl.ds(e * C, C)], preferred_element_type=F32)
                        theirs[e] = d if theirs[e] is None else theirs[e] + d
        if not last:
            big(
                round_index + 1,
                lambda v, m: v * lax.rsqrt(jnp.sum(v * v, axis=1, keepdims=True) + 1e-06),
                theirs,
            )
        else:
            for off in range(1, G):
                to = (g + off) % G
                d = copy(
                    planb.at[pl.ds(pl.multiple_of(to * S, S), S), :], ret.at[g],
                    r_ss.at[off], r_rs.at[g], (to, r),
                )
                d.start()
                back_sends.append(d)
            ret[g] = planb[pl.ds(pl.multiple_of(g * S, S), S), :]
            weight_sends = column_start(step, part)
            weights = []

            def mean_of(v, m):
                if m == 0:
                    weights.append(column_sum(step, weight_sends))
                wide = lax.broadcasted_iota(jnp.int32, (QM, K), 0) + (c * H + m * Z * QM + z * QM)
                pick = wide == lax.broadcasted_iota(jnp.int32, (QM, K), 1)
                return v / jnp.sum(jnp.where(pick, weights[0], 0.0), axis=1, keepdims=True)

            big(ROUNDS, mean_of, theirs, assign_rows)
            means_ref[...] = cent[ROUNDS % 2].reshape(K, E).astype(F32)

    for d in count_sends + row_sends + rank_sends + back_sends:
        d.wait_send()


def on_device(G, R, embeddings, labels, init_idx):
    tok, E = embeddings.shape
    K = init_idx.shape[1]
    S = 2 * tok // G
    T = min(256, S)
    N = G * S
    Z = R // 2
    Q = K // 2 // Z
    M = 2 if Q % 32 == 0 else 1
    QM = Q // M
    A = min(64, S)
    F = min(S, A + K)
    early = [(0, A)] + cut(A, F, 128)
    pieces = early + cut(F, S, 128)
    per = len(pieces)
    dma = pltpu.SemaphoreType.DMA
    vm = pltpu.VMEM
    assign, means = pl.pallas_call(
        functools.partial(kernel, G, R, tok, E, K, S, T, A, pieces, len(early)),
        out_shape=(
            jax.ShapeDtypeStruct((tok, K), BF16),
            jax.ShapeDtypeStruct((K, E), F32),
        ),
        in_specs=[pl.BlockSpec(memory_space=pltpu.HBM)] * 3,
        out_specs=[pl.BlockSpec(memory_space=pltpu.VMEM)] * 2,
        scratch_shapes=[
            vm((1, tok), jnp.int32),
            vm((1, K), jnp.int32),
            vm((tok, E), BF16),
            vm((tok, E), BF16),
            vm((G - 1, S, E), BF16),
            vm((G, S, E), BF16),
            vm((N, K), F32),
            vm((N, K), BF16),
            vm((2, K // 2, N), BF16),
            vm((2, K // 2, E // 2), F32),
            vm((G, S, K), BF16),
            vm((tok, 1), jnp.int32),
            vm((G, 8, 128), F32),
            vm((R, -(-G // 8) * 8, 128), F32),
            vm((2, R, 1, K), F32),
            vm((M, Z * QM, E), BF16),
            vm((2, M, Z * QM, E), BF16),
            vm((M, Z, QM, E), BF16),
            vm((2, M, Z, QM, E), BF16),
            vm((2, 2, M, Z, QM, E), BF16),
            dma((tok // x_sem_rows(tok),)), dma, dma,
            dma((G * per,)), dma((G * per,)),
            dma((G,)), dma((G,)),
            dma((R,)), dma((R,)),
            dma((2, R)), dma((2, R)),
            dma((2, M)), dma((2, M)),
            dma((2, M, Z)), dma((2, M, Z)),
            dma((2, M, Z)), dma((2, M, Z)),
            dma((2, M, Z)), dma((2, M, Z)),
            dma((G,)), dma((G,)),
        ],
        compiler_params=pltpu.CompilerParams(
            collective_id=0, has_side_effects=True, vmem_limit_bytes=48 * 1024 * 1024,
        ),
    )(*[pltpu.with_memory_space_constraint(v, pltpu.HBM) for v in (embeddings, labels.reshape(1, tok), init_idx)])
    return (assign, means[None])


def solution(mesh):
    return jax.shard_map(
        functools.partial(on_device, mesh.shape["sc"], mesh.shape["rows"]),
        mesh=mesh,
        in_specs=(P(("sc", "rows"), None), P(("sc", "rows"), None), P("sc", None)),
        out_specs=(P(("sc", "rows"), None), P("sc", None, None)),
        check_vma=False,
    )
```

```python
import functools
import math

import jax
import jax.numpy as jnp
from jax import lax
from jax.experimental import pallas as pl
from jax.experimental.pallas import tpu as pltpu
from jax.sharding import PartitionSpec as P

ITERS = 3
ROUNDS = 3
MESH = pl.DeviceIdType.MESH
F32 = jnp.float32
BF16 = jnp.bfloat16


def x_sem_rows(tok):
    return min(256, tok)


def cut(first, last, size):
    return [(at, min(size, last - at)) for at in range(first, last, size)]


def kernel(
    G, R, tok, E, K, S, T, A, pieces, early_pieces,
    x_ref, labr_hbm, init_hbm,
    assign_ref, means_ref,
    labr_ref, init_ref, xin, xu, out, inc, plan, planb, lhst, acc, ret, target,
    msg, tab, cs, s1s, s1r, s2s, s2r, cent,
    x_sem, l_sem, i_sem, d_ss, d_rs, c_ss, c_rs, k_ss, k_rs, cs_ss, cs_rs,
    s1_ss, s1_rs, s2_ss, s2_rs, g_ss, g_rs, f_ss, f_rs, r_ss, r_rs,
):
    g = lax.axis_index("sc")
    r = lax.axis_index("rows")
    Z = R // 2
    H = K // 2
    Q = H // Z
    M = 2 if Q % 32 == 0 else 1
    QM = Q // M
    N = G * S
    GP = -(-G // 8) * 8
    F = pieces[early_pieces - 1][0] + pieces[early_pieces - 1][1]
    per = len(pieces)
    XT = x_sem_rows(tok)
    z = r // 2
    c = r % 2
    oc = 1 - c
    partner = z * 2 + oc

    def copy(src, dst, ss, rs, to):
        return pltpu.make_async_remote_copy(
            src_ref=src, dst_ref=dst, send_sem=ss, recv_sem=rs,
            device_id=to, device_id_type=MESH,
        )

    barrier = pltpu.get_barrier_semaphore()
    for off in range(1, R):
        pl.semaphore_signal(barrier, inc=1, device_id=(g, (r + off) % R), device_id_type=MESH)
    for off in range(1, G):
        pl.semaphore_signal(barrier, inc=1, device_id=((g + off) % G, r), device_id_type=MESH)

    small = [
        pltpu.make_async_copy(labr_hbm, labr_ref, l_sem),
        pltpu.make_async_copy(init_hbm, init_ref, i_sem),
    ]
    for d in small:
        d.start()
    for i in range(tok // XT):
        at = pl.ds(i * XT, XT)
        pltpu.make_async_copy(x_ref.at[at, :], xin.at[at, :], x_sem.at[i]).start()
    for d in small:
        d.wait()

    lanes = lax.broadcasted_iota(jnp.int32, (1, 128), 1)
    sub = lax.broadcasted_iota(jnp.int32, (128, 128), 0)
    lane = lax.broadcasted_iota(jnp.int32, (128, 128), 1)
    tri = jnp.where(sub < lane, 1.0, 0.0).astype(BF16)
    labr = labr_ref[...]
    mem = jnp.where(lax.broadcasted_iota(jnp.int32, (16, tok), 0) == labr, 1.0, 0.0)

    def before(marks):
        seen = jnp.zeros((16, 1), F32)
        places = []
        for b in range(tok // 128):
            part = marks[:, b * 128:(b + 1) * 128]
            ahead = jnp.dot(part.astype(BF16), tri, preferred_element_type=F32) + seen
            places.append(jnp.sum(ahead * mem[:, b * 128:(b + 1) * 128], axis=0, keepdims=True))
            seen = seen + jnp.sum(part, axis=1, keepdims=True)
        return jnp.concatenate(places, axis=1), seen

    place, held = before(mem)
    msg[g] = jnp.zeros((8, 128), F32)
    msg[g, 0:1, :] = jnp.sum(jnp.where(sub[:16] == lane[:16], held, 0.0), axis=0, keepdims=True)
    for i in range(K // 128):
        msg[g, 1 + i:2 + i, :] = init_ref[:, i * 128:(i + 1) * 128].astype(F32)

    pl.semaphore_wait(barrier, R - 1 + G - 1)

    count_sends = []
    for off in range(1, G):
        d = copy(msg.at[g], msg.at[g], c_ss.at[off], c_rs.at[g], ((g + off) % G, r))
        d.start()
        count_sends.append(d)

    for i in range(tok // XT):
        at = pl.ds(i * XT, XT)
        pltpu.make_async_copy(x_ref.at[at, :], xin.at[at, :], x_sem.at[i]).wait()
        v = xin[at, :].astype(F32)
        scale = lax.rsqrt(jnp.mean(v * v, axis=1, keepdims=True) + 1e-05) * (1.0 / math.sqrt(E))
        xu[at, :] = (v * scale).astype(BF16)

    row_sends = []

    def moved(chosen, start, size):
        slot = lax.broadcasted_iota(jnp.int32, (size, tok), 0) + start
        perm = jnp.concatenate([jnp.where(slot == one, 1.0, 0.0).astype(BF16) for one in chosen], axis=0)
        return jnp.dot(perm, xu[...], preferred_element_type=F32).astype(BF16)

    def send_piece(j, chosen):
        start, size = pieces[j]
        at = pl.ds(start, size)
        block = moved(chosen, start, size)
        for off in range(1, G):
            out[off - 1, at, :] = block[(off - 1) * size:off * size]
            d = copy(
                out.at[off - 1, at, :], inc.at[g, at, :],
                d_ss.at[off * per + j], d_rs.at[g * per + j], ((g + off) % G, r),
            )
            d.start()
            row_sends.append(d)

    def wait_piece(j):
        for off in range(1, G):
            src = (g + off) % G
            part = inc.at[src, pl.ds(*pieces[j]), :]
            copy(part, part, d_ss.at[off * per + j], d_rs.at[src * per + j], (src, r)).wait_recv()

    def chosen_of(place_i):
        return [jnp.where(labr == (g + off) % G, place_i, -1) for off in range(1, G + 1)]

    send_piece(0, chosen_of(place.astype(jnp.int32))[:G - 1])

    for off in range(1, G):
        src = (g + off) % G
        copy(msg.at[src], msg.at[src], c_ss.at[off], c_rs.at[src], (src, r)).wait_recv()
    tab[r] = jnp.zeros((GP, 128), F32)
    for q in range(G):
        tab[r, q:q + 1, :] = msg[q, 0:1, :]
    rank_sends = []
    for off in range(1, R):
        to = (r + off) % R
        d = copy(tab.at[r], tab.at[r], k_ss.at[off], k_rs.at[r], (g, to))
        d.start()
        rank_sends.append(d)
    for off in range(1, R):
        src = (r + off) % R
        copy(tab.at[src], tab.at[src], k_ss.at[off], k_rs.at[src], (g, src)).wait_recv()
    totals = jnp.zeros((GP, 128), F32)
    early = jnp.zeros((GP, 128), F32)
    for q in range(R):
        rows = tab[q]
        totals = totals + rows
        early = early + jnp.where(r > q, rows, 0.0)
    total = jnp.sum(totals, axis=0, keepdims=True)
    where_g = lax.broadcasted_iota(jnp.int32, (GP, 128), 0)
    ahead = jnp.sum(
        jnp.where(where_g < g, totals, 0.0) + jnp.where(where_g == g, early, 0.0), axis=0, keepdims=True
    )

    def at_lane(row, q):
        return jnp.sum(jnp.where(lanes == q, row, 0.0), axis=1, keepdims=True)

    def upright(row):
        return jnp.broadcast_to(row, (128, row.shape[1])).T[:, :1]

    def wanted_of(q):
        count = at_lane(total, q)
        asked = jnp.concatenate([msg[q, 1 + i:2 + i, :] for i in range(K // 128)], axis=1)
        return asked - jnp.floor((asked + 0.5) / count) * count

    span = 2.0 * G * R * S
    key = place
    for q in range(G):
        key = key + jnp.where(labr == q, at_lane(ahead, q) + q * span, 0.0)
    hits = jnp.zeros((8, tok), F32)
    for q in range(G):
        same = jnp.where(upright(wanted_of(q) + q * span) == key, 1.0, 0.0)
        hits = hits + jnp.sum(same.reshape(K // 8, 8, tok), axis=0)
    hit = (jnp.sum(hits, axis=0, keepdims=True) > 0.0) & (place >= A)
    seeds = jnp.where(hit, mem, 0.0)
    seed_place, seed_count = before(seeds)
    seeds_all = jnp.sum(seed_count * mem, axis=0, keepdims=True)
    place = jnp.where(
        place < A, place, jnp.where(hit, seed_place + A, place + seeds_all - seed_place)
    )
    chosen = chosen_of(place.astype(jnp.int32))
    for j in range(1, per):
        send_piece(j, chosen[:G - 1])
    for i in range(S // T):
        inc[g, pl.ds(i * T, T), :] = moved(chosen[G - 1:], i * T, T)

    slot_of = labr.astype(F32) * S + place
    for b in range(tok // 128):
        wide = jnp.broadcast_to(slot_of[:, b * 128:(b + 1) * 128], (128, 128))
        target[pl.ds(b * 128, 128), :] = wide.T[:, :1].astype(jnp.int32)

    mine = jnp.where(lax.broadcasted_iota(jnp.int32, (GP, 128), 1) == g, 1.0, 0.0)
    totals_g = jnp.sum(totals * mine, axis=1, keepdims=True)
    early_g = jnp.sum(early * mine, axis=1, keepdims=True)
    here_g = jnp.sum(tab[r] * mine, axis=1, keepdims=True)
    n_here = [here_g[q:q + 1] for q in range(G)]
    wide_w = wanted_of(g)
    tall_w = upright(wide_w)
    before_k = lax.broadcasted_iota(jnp.int32, (K, K), 0) < lax.broadcasted_iota(jnp.int32, (K, K), 1)
    again = jnp.max(jnp.where((tall_w == wide_w) & before_k, 1.0, 0.0), axis=0, keepdims=True)
    lower = jnp.sum(jnp.where(wide_w < tall_w, 1.0 - again, 0.0), axis=1, keepdims=True)
    slots = lax.broadcasted_iota(jnp.int32, (1, F), 1).astype(F32)
    base = jnp.zeros((1, 1), F32)
    for q in range(G):
        start = base + early_g[q:q + 1]
        base = base + totals_g[q:q + 1]
        local = tall_w - start
        fewer = jnp.sum(jnp.where(wide_w < start + A, 1.0 - again, 0.0), axis=1, keepdims=True)
        slot = jnp.where(local < A, local, lower - fewer + A)
        slot = jnp.where((local >= 0.0) & (local < n_here[q]), slot, -1.0)
        pick = jnp.where(slot == slots, 1.0, 0.0).astype(BF16)
        lhst[0, :, pl.ds(q * S, F)] = pick[:H]
        lhst[1, :, pl.ds(q * S, F)] = pick[H:]

    for j in range(early_pieces):
        wait_piece(j)

    C = E // 2
    pending = []

    def half_sum(h, e):
        rows = inc[:, :, pl.ds(e * C, C)].reshape(N, C)
        return jnp.dot(lhst[h], rows, preferred_element_type=F32)

    def seed_sum(h, e):
        total = None
        for q in range(G):
            part = jnp.dot(
                lhst[h, :, pl.ds(q * S, F)], inc[q, pl.ds(0, F), pl.ds(e * C, C)],
                preferred_element_type=F32,
            )
            total = part if total is None else total + part
        return total

    def big(t, finish, theirs, meanwhile=None, half_sum=half_sum):
        slot = t % 2
        first = []
        sends = []
        for m in range(M):
            for e in range(2):
                s1s[m, :, pl.ds(e * C, C)] = theirs[e][m * Z * QM:(m + 1) * Z * QM].astype(BF16)
            d = copy(s1s.at[m], s1r.at[slot, m], s1_ss.at[slot, m], s1_rs.at[slot, m], (g, partner))
            d.start()
            first.append(d)
        for e in range(2):
            acc[e] = half_sum(c, e)
        for m in range(M):
            at = pl.ds(m * Z * QM, Z * QM)
            first[m].wait_recv()
            for e in range(2):
                both = acc[e, at, :] + s1r[slot, m, :, pl.ds(e * C, C)].astype(F32)
                acc[e, at, :] = both
                s2s[m, :, :, pl.ds(e * C, C)] = both.astype(BF16).reshape(Z, QM, C)
            for off in range(1, Z):
                to = (z + off) % Z
                d = copy(
                    s2s.at[m, to], s2r.at[slot, m, z],
                    s2_ss.at[slot, m, off], s2_rs.at[slot, m, z], (g, to * 2 + c),
                )
                d.start()
                sends.append(d)
        for m in range(M):
            at = pl.ds(pl.multiple_of(m * Z * QM + z * QM, QM), QM)
            own = jnp.concatenate([acc[0, at, :], acc[1, at, :]], axis=1)
            for off in range(1, Z):
                src = (z + off) % Z
                part = s2r.at[slot, m, src]
                copy(
                    part, part, s2_ss.at[slot, m, off], s2_rs.at[slot, m, src], (g, src * 2 + c)
                ).wait_recv()
                own = own + s2r[slot, m, src].astype(F32)
            mine = cent.at[slot, c, m, z]
            cent[slot, c, m, z] = finish(own, m).astype(BF16)
            for off in range(1, Z):
                to = (z + off) % Z
                d = copy(mine, mine, g_ss.at[slot, m, off], g_rs.at[slot, m, z], (g, to * 2 + c))
                d.start()
                sends.append(d)
            d = copy(mine, mine, f_ss.at[slot, m, z], f_rs.at[slot, m, z], (g, partner))
            d.start()
            sends.append(d)
        if meanwhile is not None:
            meanwhile()
        for m in range(M):
            for off in range(1, Z):
                src = (z + off) % Z
                part = cent.at[slot, c, m, src]
                copy(part, part, g_ss.at[slot, m, off], g_rs.at[slot, m, src], (g, src * 2 + c)).wait_recv()
                d = copy(part, part, f_ss.at[slot, m, src], f_rs.at[slot, m, src], (g, partner))
                d.start()
                sends.append(d)
        for m in range(M):
            for off in range(Z):
                src = (z + off) % Z
                part = cent.at[slot, oc, m, src]
                copy(part, part, f_ss.at[slot, m, src], f_rs.at[slot, m, src], (g, partner)).wait_recv()
        pending.extend(first + sends)

    def column_start(t, part8):
        slot = t % 2
        cs[slot, r] = jnp.sum(part8, axis=0, keepdims=True)
        sends = []
        for off in sorted(range(1, R), key=lambda o: -min(o, R - o)):
            to = (r + off) % R
            d = copy(cs.at[slot, r], cs.at[slot, r], cs_ss.at[slot, off], cs_rs.at[slot, r], (g, to))
            d.start()
            sends.append(d)
        for d in pending:
            d.wait_send()
        pending[:] = sends
        return sends

    def column_sum(t, sends):
        slot = t % 2
        for off in range(1, R):
            src = (r + off) % R
            part = cs.at[slot, src]
            copy(part, part, cs_ss.at[slot, off], cs_rs.at[slot, src], (g, src)).wait_recv()
        whole = cs[slot, 0]
        for q in range(1, R):
            whole = whole + cs[slot, q]
        return whole

    tiles = N // T
    zero8 = jnp.zeros((8, K), F32)

    def down(v):
        return jnp.sum(v.reshape(v.shape[0] // 8, 8, K), axis=0)

    def assign_rows():
        for off in range(1, G):
            src = (g + off) % G
            part = ret.at[src]
            copy(part, part, r_ss.at[off], r_rs.at[src], (src, r)).wait_recv()

        def one(i, carry):
            at = pl.ds(pl.multiple_of(i * 256, 256), 256)
            hot = jnp.where(
                lax.broadcasted_iota(jnp.int32, (256, N), 1) == target[at, :], 1.0, 0.0
            ).astype(BF16)
            assign_ref[at, :] = jnp.dot(
                hot, ret[...].reshape(N, K), preferred_element_type=F32
            ).astype(BF16)
            return carry

        lax.fori_loop(0, tok // 256, one, 0)

    big(0, lambda v, m: v, [seed_sum(oc, e) for e in range(2)], None, seed_sum)
    step = 0
    back_sends = []
    for round_index in range(ROUNDS):
        last = round_index == ROUNDS - 1
        slot = round_index % 2
        part = zero8
        areas = [(0, F)] + pieces[early_pieces:] if round_index == 0 else [(0, S)]
        for j, (start, size) in enumerate(areas):
            if round_index == 0 and j > 0:
                wait_piece(early_pieces + j - 1)
            for q in range(G):
                v = lax.dot_general(
                    inc[q, pl.ds(start, size), :], cent[slot].reshape(K, E),
                    (((1,), (1,)), ((), ())), preferred_element_type=F32,
                )
                at = (lax.broadcasted_iota(jnp.int32, (size, 1), 0) + start).astype(F32)
                v = jnp.where(at < n_here[q], jnp.exp(v * 10.0), 0.0)
                plan[pl.ds(q * S + start, size), :] = v
                part = part + down(v)
        for it in range(ITERS):
            col = 1.0 / column_sum(step, column_start(step, part))
            step += 1
            part = zero8
            if it < ITERS - 1:
                for i in range(tiles):
                    v = plan[pl.ds(i * T, T), :]
                    s = jnp.sum(v * col, axis=1, keepdims=True)
                    part = part + down(v * jnp.where(s > 0.0, 1.0 / s, 0.0))
            else:
                theirs = [None, None]
                for q in range(G):
                    at = pl.ds(q * S, S)
                    v = plan[at, :] * col
                    s = jnp.sum(v, axis=1, keepdims=True)
                    v = v * jnp.where(s > 0.0, 1.0 / s, 0.0)
                    if last:
                        planb[at, :] = v.astype(BF16)
                        part = part + down(v)
                    vt = v.T.astype(BF16)
                    lhst[0, :, at] = vt[:H]
                    lhst[1, :, at] = vt[H:]
                    vo = jnp.where(c == 0, vt[H:], vt[:H])
                    for e in range(2):
                        d = jnp.dot(vo, inc[q, :, pl.ds(e * C, C)], preferred_element_type=F32)
                        theirs[e] = d if theirs[e] is None else theirs[e] + d
        if not last:
            big(
                round_index + 1,
                lambda v, m: v * lax.rsqrt(jnp.sum(v * v, axis=1, keepdims=True) + 1e-06),
                theirs,
            )
        else:
            for off in range(1, G):
                to = (g + off) % G
                d = copy(
                    planb.at[pl.ds(pl.multiple_of(to * S, S), S), :], ret.at[g],
                    r_ss.at[off], r_rs.at[g], (to, r),
                )
                d.start()
                back_sends.append(d)
            ret[g] = planb[pl.ds(pl.multiple_of(g * S, S), S), :]
            weight_sends = column_start(step, part)
            weights = []

            def mean_of(v, m):
                if m == 0:
                    weights.append(column_sum(step, weight_sends))
                wide = lax.broadcasted_iota(jnp.int32, (QM, K), 0) + (c * H + m * Z * QM + z * QM)
                pick = wide == lax.broadcasted_iota(jnp.int32, (QM, K), 1)
                return v / jnp.sum(jnp.where(pick, weights[0], 0.0), axis=1, keepdims=True)

            big(ROUNDS, mean_of, theirs, assign_rows)
            means_ref[...] = cent[ROUNDS % 2].reshape(K, E).astype(F32)

    for d in pending + count_sends + row_sends + rank_sends + back_sends:
        d.wait_send()


def on_device(G, R, embeddings, labels, init_idx):
    tok, E = embeddings.shape
    K = init_idx.shape[1]
    S = 2 * tok // G
    T = min(256, S)
    N = G * S
    Z = R // 2
    Q = K // 2 // Z
    M = 2 if Q % 32 == 0 else 1
    QM = Q // M
    A = min(64, S)
    F = min(S, A + K)
    early = [(0, A)] + cut(A, F, 128)
    pieces = early + cut(F, S, 128)
    per = len(pieces)
    dma = pltpu.SemaphoreType.DMA
    vm = pltpu.VMEM
    assign, means = pl.pallas_call(
        functools.partial(kernel, G, R, tok, E, K, S, T, A, pieces, len(early)),
        out_shape=(
            jax.ShapeDtypeStruct((tok, K), BF16),
            jax.ShapeDtypeStruct((K, E), F32),
        ),
        in_specs=[pl.BlockSpec(memory_space=pltpu.HBM)] * 3,
        out_specs=[pl.BlockSpec(memory_space=pltpu.VMEM)] * 2,
        scratch_shapes=[
            vm((1, tok), jnp.int32),
            vm((1, K), jnp.int32),
            vm((tok, E), BF16),
            vm((tok, E), BF16),
            vm((G - 1, S, E), BF16),
            vm((G, S, E), BF16),
            vm((N, K), F32),
            vm((N, K), BF16),
            vm((2, K // 2, N), BF16),
            vm((2, K // 2, E // 2), F32),
            vm((G, S, K), BF16),
            vm((tok, 1), jnp.int32),
            vm((G, 8, 128), F32),
            vm((R, -(-G // 8) * 8, 128), F32),
            vm((2, R, 1, K), F32),
            vm((M, Z * QM, E), BF16),
            vm((2, M, Z * QM, E), BF16),
            vm((M, Z, QM, E), BF16),
            vm((2, M, Z, QM, E), BF16),
            vm((2, 2, M, Z, QM, E), BF16),
            dma((tok // x_sem_rows(tok),)), dma, dma,
            dma((G * per,)), dma((G * per,)),
            dma((G,)), dma((G,)),
            dma((R,)), dma((R,)),
            dma((2, R)), dma((2, R)),
            dma((2, M)), dma((2, M)),
            dma((2, M, Z)), dma((2, M, Z)),
            dma((2, M, Z)), dma((2, M, Z)),
            dma((2, M, Z)), dma((2, M, Z)),
            dma((G,)), dma((G,)),
        ],
        compiler_params=pltpu.CompilerParams(
            collective_id=0, has_side_effects=True, vmem_limit_bytes=48 * 1024 * 1024,
        ),
    )(*[pltpu.with_memory_space_constraint(v, pltpu.HBM) for v in (embeddings, labels.reshape(1, tok), init_idx)])
    return (assign, means[None])


def solution(mesh):
    return jax.shard_map(
        functools.partial(on_device, mesh.shape["sc"], mesh.shape["rows"]),
        mesh=mesh,
        in_specs=(P(("sc", "rows"), None), P(("sc", "rows"), None), P("sc", None)),
        out_specs=(P(("sc", "rows"), None), P("sc", None, None)),
        check_vma=False,
    )
```

```python
import functools
import math

import jax
import jax.numpy as jnp
from jax import lax
from jax.experimental import pallas as pl
from jax.experimental.pallas import tpu as pltpu
from jax.sharding import PartitionSpec as P

ITERS = 3
ROUNDS = 3
MESH = pl.DeviceIdType.MESH
F32 = jnp.float32
BF16 = jnp.bfloat16


def x_sem_rows(tok):
    return min(256, tok)


def cut(first, last, size):
    return [(at, min(size, last - at)) for at in range(first, last, size)]


def kernel(
    G, R, tok, E, K, S, T, A, pieces, early_pieces,
    x_ref, labr_hbm, init_hbm,
    assign_ref, means_ref,
    labr_ref, init_ref, xin, xu, out, inc, plan, planb, lhst, acc, ret, target,
    msg, tab, tall, cs, s1s, s1r, s2s, s2r, cent,
    x_sem, l_sem, i_sem, d_ss, d_rs, c_ss, c_rs, k_ss, k_rs, cs_ss, cs_rs,
    s1_ss, s1_rs, s2_ss, s2_rs, g_ss, g_rs, f_ss, f_rs, r_ss, r_rs,
):
    g = lax.axis_index("sc")
    r = lax.axis_index("rows")
    Z = R // 2
    H = K // 2
    Q = H // Z
    M = 2 if Q % 32 == 0 else 1
    QM = Q // M
    N = G * S
    GP = -(-G // 8) * 8
    F = pieces[early_pieces - 1][0] + pieces[early_pieces - 1][1]
    per = len(pieces)
    XT = x_sem_rows(tok)
    z = r // 2
    c = r % 2
    half = (c + z) % 2
    oc = 1 - half
    partner = z * 2 + 1 - c

    def copy(src, dst, ss, rs, to):
        return pltpu.make_async_remote_copy(
            src_ref=src, dst_ref=dst, send_sem=ss, recv_sem=rs,
            device_id=to, device_id_type=MESH,
        )

    barrier = pltpu.get_barrier_semaphore()
    for off in range(1, R):
        pl.semaphore_signal(barrier, inc=1, device_id=(g, (r + off) % R), device_id_type=MESH)
    for off in range(1, G):
        pl.semaphore_signal(barrier, inc=1, device_id=((g + off) % G, r), device_id_type=MESH)

    small = [
        pltpu.make_async_copy(labr_hbm, labr_ref, l_sem),
        pltpu.make_async_copy(init_hbm, init_ref, i_sem),
    ]
    for d in small:
        d.start()
    for i in range(tok // XT):
        at = pl.ds(i * XT, XT)
        pltpu.make_async_copy(x_ref.at[at, :], xin.at[at, :], x_sem.at[i]).start()
    for d in small:
        d.wait()

    lanes = lax.broadcasted_iota(jnp.int32, (1, 128), 1)
    sub = lax.broadcasted_iota(jnp.int32, (128, 128), 0)
    lane = lax.broadcasted_iota(jnp.int32, (128, 128), 1)
    tri = jnp.where(sub < lane, 1.0, 0.0).astype(BF16)
    labr = labr_ref[...]
    mem = jnp.where(lax.broadcasted_iota(jnp.int32, (16, tok), 0) == labr, 1.0, 0.0)

    def before(marks):
        seen = jnp.zeros((16, 1), F32)
        places = []
        for b in range(tok // 128):
            part = marks[:, b * 128:(b + 1) * 128]
            ahead = jnp.dot(part.astype(BF16), tri, preferred_element_type=F32) + seen
            places.append(jnp.sum(ahead * mem[:, b * 128:(b + 1) * 128], axis=0, keepdims=True))
            seen = seen + jnp.sum(part, axis=1, keepdims=True)
        return jnp.concatenate(places, axis=1), seen

    held = jnp.sum(mem, axis=1, keepdims=True)
    msg[g] = jnp.zeros((8, 128), F32)
    msg[g, 0:1, :] = jnp.sum(jnp.where(sub[:16] == lane[:16], held, 0.0), axis=0, keepdims=True)
    for i in range(K // 128):
        msg[g, 1 + i:2 + i, :] = init_ref[:, i * 128:(i + 1) * 128].astype(F32)

    pl.semaphore_wait(barrier, R - 1 + G - 1)

    count_sends = []
    for off in range(1, G):
        d = copy(msg.at[g], msg.at[g], c_ss.at[off], c_rs.at[g], ((g + off) % G, r))
        d.start()
        count_sends.append(d)

    for i in range(tok // XT):
        at = pl.ds(i * XT, XT)
        pltpu.make_async_copy(x_ref.at[at, :], xin.at[at, :], x_sem.at[i]).wait()
        v = xin[at, :].astype(F32)
        scale = lax.rsqrt(jnp.mean(v * v, axis=1, keepdims=True) + 1e-05) * (1.0 / math.sqrt(E))
        xu[at, :] = (v * scale).astype(BF16)

    place, _ = before(mem)
    row_sends = []

    def moved(chosen, start, size):
        slot = lax.broadcasted_iota(jnp.int32, (size, tok), 0) + start
        perm = jnp.concatenate([jnp.where(slot == one, 1.0, 0.0).astype(BF16) for one in chosen], axis=0)
        return jnp.dot(perm, xu[...], preferred_element_type=F32).astype(BF16)

    def send_piece(j, chosen):
        start, size = pieces[j]
        at = pl.ds(start, size)
        block = moved(chosen, start, size)
        for off in range(1, G):
            out[off - 1, at, :] = block[(off - 1) * size:off * size]
            d = copy(
                out.at[off - 1, at, :], inc.at[g, at, :],
                d_ss.at[off * per + j], d_rs.at[g * per + j], ((g + off) % G, r),
            )
            d.start()
            row_sends.append(d)

    def wait_piece(j):
        for off in range(1, G):
            src = (g + off) % G
            part = inc.at[src, pl.ds(*pieces[j]), :]
            copy(part, part, d_ss.at[off * per + j], d_rs.at[src * per + j], (src, r)).wait_recv()

    def chosen_of(place_i):
        return [jnp.where(labr == (g + off) % G, place_i, -1) for off in range(1, G + 1)]

    send_piece(0, chosen_of(place.astype(jnp.int32))[:G - 1])

    for off in range(1, G):
        src = (g + off) % G
        copy(msg.at[src], msg.at[src], c_ss.at[off], c_rs.at[src], (src, r)).wait_recv()
    tab[r] = jnp.zeros((GP, 128), F32)
    for q in range(G):
        tab[r, q:q + 1, :] = msg[q, 0:1, :]
    rank_sends = []
    for off in range(1, R):
        to = (r + off) % R
        d = copy(tab.at[r], tab.at[r], k_ss.at[off], k_rs.at[r], (g, to))
        d.start()
        rank_sends.append(d)
    def asked_of(q):
        return jnp.concatenate([msg[q, 1 + i:2 + i, :] for i in range(K // 128)], axis=1)

    for q in range(G):
        tall[q] = jnp.broadcast_to(asked_of(q), (128, K)).T
    for off in range(1, R):
        src = (r + off) % R
        copy(tab.at[src], tab.at[src], k_ss.at[off], k_rs.at[src], (g, src)).wait_recv()
    totals = jnp.zeros((GP, 128), F32)
    early = jnp.zeros((GP, 128), F32)
    for q in range(R):
        rows = tab[q]
        totals = totals + rows
        early = early + jnp.where(r > q, rows, 0.0)
    total = jnp.sum(totals, axis=0, keepdims=True)
    where_g = lax.broadcasted_iota(jnp.int32, (GP, 128), 0)
    ahead = jnp.sum(
        jnp.where(where_g < g, totals, 0.0) + jnp.where(where_g == g, early, 0.0), axis=0, keepdims=True
    )

    def at_lane(row, q):
        return jnp.sum(jnp.where(lanes == q, row, 0.0), axis=1, keepdims=True)

    def wanted_of(q, asked):
        count = at_lane(total, q)
        return asked - jnp.floor((asked + 0.5) / count) * count

    span = 2.0 * G * R * S
    key = place
    for q in range(G):
        key = key + jnp.where(labr == q, at_lane(ahead, q) + q * span, 0.0)
    hits = jnp.zeros((8, tok), F32)
    for q in range(G):
        goal = wanted_of(q, tall[q]) + q * span
        hits = hits + jnp.concatenate([
            jnp.sum(
                jnp.where(goal == key[:, b * 128:(b + 1) * 128], 1.0, 0.0).reshape(K // 8, 8, 128), axis=0
            )
            for b in range(tok // 128)
        ], axis=1)
    hit = (jnp.sum(hits, axis=0, keepdims=True) > 0.0) & (place >= A)
    seeds = jnp.where(hit, mem, 0.0)
    seed_place, seed_count = before(seeds)
    seeds_all = jnp.sum(seed_count * mem, axis=0, keepdims=True)
    place = jnp.where(
        place < A, place, jnp.where(hit, seed_place + A, place + seeds_all - seed_place)
    )
    chosen = chosen_of(place.astype(jnp.int32))
    for j in range(1, per):
        send_piece(j, chosen[:G - 1])
    for i in range(S // T):
        inc[g, pl.ds(i * T, T), :] = moved(chosen[G - 1:], i * T, T)

    slot_of = labr.astype(F32) * S + place
    for b in range(tok // 128):
        wide = jnp.broadcast_to(slot_of[:, b * 128:(b + 1) * 128], (128, 128))
        target[pl.ds(b * 128, 128), :] = wide.T[:, :1].astype(jnp.int32)

    mine = jnp.where(lax.broadcasted_iota(jnp.int32, (GP, 128), 1) == g, 1.0, 0.0)
    totals_g = jnp.sum(totals * mine, axis=1, keepdims=True)
    early_g = jnp.sum(early * mine, axis=1, keepdims=True)
    here_g = jnp.sum(tab[r] * mine, axis=1, keepdims=True)
    n_here = [here_g[q:q + 1] for q in range(G)]
    wide_w = wanted_of(g, asked_of(g))
    tall_w = wanted_of(g, tall[g])[:, :1]
    before_k = lax.broadcasted_iota(jnp.int32, (K, K), 0) < lax.broadcasted_iota(jnp.int32, (K, K), 1)
    again = jnp.max(jnp.where((tall_w == wide_w) & before_k, 1.0, 0.0), axis=0, keepdims=True)
    lower = jnp.sum(jnp.where(wide_w < tall_w, 1.0 - again, 0.0), axis=1, keepdims=True)
    slots = lax.broadcasted_iota(jnp.int32, (1, F), 1).astype(F32)
    base = jnp.zeros((1, 1), F32)
    for q in range(G):
        start = base + early_g[q:q + 1]
        base = base + totals_g[q:q + 1]
        local = tall_w - start
        fewer = jnp.sum(jnp.where(wide_w < start + A, 1.0 - again, 0.0), axis=1, keepdims=True)
        slot = jnp.where(local < A, local, lower - fewer + A)
        slot = jnp.where((local >= 0.0) & (local < n_here[q]), slot, -1.0)
        pick = jnp.where(slot == slots, 1.0, 0.0).astype(BF16)
        lhst[0, :, pl.ds(q * S, F)] = pick[:H]
        lhst[1, :, pl.ds(q * S, F)] = pick[H:]

    for j in range(early_pieces):
        wait_piece(j)

    C = E // 2
    pending = []

    def half_sum(h, e):
        rows = inc[:, :, pl.ds(e * C, C)].reshape(N, C)
        return jnp.dot(lhst[h], rows, preferred_element_type=F32)

    def seed_sum(h, e):
        total = None
        for q in range(G):
            part = jnp.dot(
                lhst[h, :, pl.ds(q * S, F)], inc[q, pl.ds(0, F), pl.ds(e * C, C)],
                preferred_element_type=F32,
            )
            total = part if total is None else total + part
        return total

    def big(t, finish, theirs, meanwhile=None, half_sum=half_sum):
        slot = t % 2
        first = []
        sends = []
        for m in range(M):
            for e in range(2):
                s1s[m, :, pl.ds(e * C, C)] = theirs[e][m * Z * QM:(m + 1) * Z * QM].astype(BF16)
            d = copy(s1s.at[m], s1r.at[slot, m], s1_ss.at[slot, m], s1_rs.at[slot, m], (g, partner))
            d.start()
            first.append(d)
        for e in range(2):
            acc[e] = half_sum(half, e)
        for m in range(M):
            at = pl.ds(m * Z * QM, Z * QM)
            first[m].wait_recv()
            for e in range(2):
                both = acc[e, at, :] + s1r[slot, m, :, pl.ds(e * C, C)].astype(F32)
                acc[e, at, :] = both
                s2s[m, :, :, pl.ds(e * C, C)] = both.astype(BF16).reshape(Z, QM, C)
            for off in range(1, Z):
                to = (z + off) % Z
                d = copy(
                    s2s.at[m, to], s2r.at[slot, m, z],
                    s2_ss.at[slot, m, off], s2_rs.at[slot, m, z], (g, to * 2 + (half + to) % 2),
                )
                d.start()
                sends.append(d)
        for m in range(M):
            at = pl.ds(pl.multiple_of(m * Z * QM + z * QM, QM), QM)
            own = jnp.concatenate([acc[0, at, :], acc[1, at, :]], axis=1)
            for off in range(1, Z):
                src = (z + off) % Z
                part = s2r.at[slot, m, src]
                copy(
                    part, part, s2_ss.at[slot, m, off], s2_rs.at[slot, m, src], (g, src * 2 + (half + src) % 2)
                ).wait_recv()
                own = own + s2r[slot, m, src].astype(F32)
            mine = cent.at[slot, half, m, z]
            cent[slot, half, m, z] = finish(own, m).astype(BF16)
            for off in range(1, Z):
                to = (z + off) % Z
                d = copy(mine, mine, g_ss.at[slot, m, off], g_rs.at[slot, m, z], (g, to * 2 + (half + to) % 2))
                d.start()
                sends.append(d)
            d = copy(mine, mine, f_ss.at[slot, m, z], f_rs.at[slot, m, z], (g, partner))
            d.start()
            sends.append(d)
        if meanwhile is not None:
            meanwhile()
        for m in range(M):
            for off in range(1, Z):
                src = (z + off) % Z
                part = cent.at[slot, half, m, src]
                copy(part, part, g_ss.at[slot, m, off], g_rs.at[slot, m, src], (g, src * 2 + (half + src) % 2)).wait_recv()
                d = copy(part, part, f_ss.at[slot, m, src], f_rs.at[slot, m, src], (g, partner))
                d.start()
                sends.append(d)
        for m in range(M):
            for off in range(Z):
                src = (z + off) % Z
                part = cent.at[slot, oc, m, src]
                copy(part, part, f_ss.at[slot, m, src], f_rs.at[slot, m, src], (g, partner)).wait_recv()
        pending.extend(first + sends)

    def column_start(t, part8):
        slot = t % 2
        cs[slot, r] = jnp.sum(part8, axis=0, keepdims=True)
        sends = []
        for off in sorted(range(1, R), key=lambda o: -min(o, R - o)):
            to = (r + off) % R
            d = copy(cs.at[slot, r], cs.at[slot, r], cs_ss.at[slot, off], cs_rs.at[slot, r], (g, to))
            d.start()
            sends.append(d)
        for d in pending:
            d.wait_send()
        pending[:] = sends
        return sends

    def column_sum(t, sends):
        slot = t % 2
        for off in range(1, R):
            src = (r + off) % R
            part = cs.at[slot, src]
            copy(part, part, cs_ss.at[slot, off], cs_rs.at[slot, src], (g, src)).wait_recv()
        whole = cs[slot, 0]
        for q in range(1, R):
            whole = whole + cs[slot, q]
        return whole

    tiles = N // T
    zero8 = jnp.zeros((8, K), F32)

    def down(v):
        return jnp.sum(v.reshape(v.shape[0] // 8, 8, K), axis=0)

    def assign_rows():
        for off in range(1, G):
            src = (g + off) % G
            part = ret.at[src]
            copy(part, part, r_ss.at[off], r_rs.at[src], (src, r)).wait_recv()

        def one(i, carry):
            at = pl.ds(pl.multiple_of(i * 256, 256), 256)
            hot = jnp.where(
                lax.broadcasted_iota(jnp.int32, (256, N), 1) == target[at, :], 1.0, 0.0
            ).astype(BF16)
            assign_ref[at, :] = jnp.dot(
                hot, ret[...].reshape(N, K), preferred_element_type=F32
            ).astype(BF16)
            return carry

        lax.fori_loop(0, tok // 256, one, 0)

    big(0, lambda v, m: v, [seed_sum(oc, e) for e in range(2)], None, seed_sum)
    step = 0
    back_sends = []
    for round_index in range(ROUNDS):
        last = round_index == ROUNDS - 1
        slot = round_index % 2
        part = zero8
        areas = [(0, F)] + [(F, S - F)] * (F < S) if round_index == 0 else [(0, S)]
        for j, (start, size) in enumerate(areas):
            if round_index == 0 and j > 0:
                for piece in range(early_pieces, per):
                    wait_piece(piece)
            for q in range(G):
                v = lax.dot_general(
                    inc[q, pl.ds(start, size), :], cent[slot].reshape(K, E),
                    (((1,), (1,)), ((), ())), preferred_element_type=F32,
                )
                at = (lax.broadcasted_iota(jnp.int32, (size, 1), 0) + start).astype(F32)
                v = jnp.where(at < n_here[q], jnp.exp(v * 10.0), 0.0)
                plan[pl.ds(q * S + start, size), :] = v
                part = part + down(v)
        for it in range(ITERS):
            col = 1.0 / column_sum(step, column_start(step, part))
            step += 1
            part = zero8
            if it < ITERS - 1:
                for i in range(tiles):
                    v = plan[pl.ds(i * T, T), :]
                    s = jnp.sum(v * col, axis=1, keepdims=True)
                    part = part + down(v * jnp.where(s > 0.0, 1.0 / s, 0.0))
            else:
                theirs = [None, None]
                for q in range(G):
                    at = pl.ds(q * S, S)
                    v = plan[at, :] * col
                    s = jnp.sum(v, axis=1, keepdims=True)
                    v = v * jnp.where(s > 0.0, 1.0 / s, 0.0)
                    if last:
                        planb[at, :] = v.astype(BF16)
                        part = part + down(v)
                    vt = v.T.astype(BF16)
                    lhst[0, :, at] = vt[:H]
                    lhst[1, :, at] = vt[H:]
                    vo = jnp.where(half == 0, vt[H:], vt[:H])
                    for e in range(2):
                        d = jnp.dot(vo, inc[q, :, pl.ds(e * C, C)], preferred_element_type=F32)
                        theirs[e] = d if theirs[e] is None else theirs[e] + d
        if not last:
            big(
                round_index + 1,
                lambda v, m: v * lax.rsqrt(jnp.sum(v * v, axis=1, keepdims=True) + 1e-06),
                theirs,
            )
        else:
            for off in range(1, G):
                to = (g + off) % G
                d = copy(
                    planb.at[pl.ds(pl.multiple_of(to * S, S), S), :], ret.at[g],
                    r_ss.at[off], r_rs.at[g], (to, r),
                )
                d.start()
                back_sends.append(d)
            ret[g] = planb[pl.ds(pl.multiple_of(g * S, S), S), :]
            weight_sends = column_start(step, part)
            weights = []

            def mean_of(v, m):
                if m == 0:
                    weights.append(column_sum(step, weight_sends))
                wide = lax.broadcasted_iota(jnp.int32, (QM, K), 0) + (half * H + m * Z * QM + z * QM)
                pick = wide == lax.broadcasted_iota(jnp.int32, (QM, K), 1)
                return v / jnp.sum(jnp.where(pick, weights[0], 0.0), axis=1, keepdims=True)

            big(ROUNDS, mean_of, theirs, assign_rows)
            means_ref[...] = cent[ROUNDS % 2].reshape(K, E).astype(F32)

    for d in pending + count_sends + row_sends + rank_sends + back_sends:
        d.wait_send()


def on_device(G, R, embeddings, labels, init_idx):
    tok, E = embeddings.shape
    K = init_idx.shape[1]
    S = 2 * tok // G
    T = min(256, S)
    N = G * S
    Z = R // 2
    Q = K // 2 // Z
    M = 2 if Q % 32 == 0 else 1
    QM = Q // M
    A = min(64, S)
    F = min(S, A + K)
    early = [(0, A)] + cut(A, F, 128)
    pieces = early + cut(F, S, 128)
    per = len(pieces)
    dma = pltpu.SemaphoreType.DMA
    vm = pltpu.VMEM
    assign, means = pl.pallas_call(
        functools.partial(kernel, G, R, tok, E, K, S, T, A, pieces, len(early)),
        out_shape=(
            jax.ShapeDtypeStruct((tok, K), BF16),
            jax.ShapeDtypeStruct((K, E), F32),
        ),
        in_specs=[pl.BlockSpec(memory_space=pltpu.HBM)] * 3,
        out_specs=[pl.BlockSpec(memory_space=pltpu.VMEM)] * 2,
        scratch_shapes=[
            vm((1, tok), jnp.int32),
            vm((1, K), jnp.int32),
            vm((tok, E), BF16),
            vm((tok, E), BF16),
            vm((G - 1, S, E), BF16),
            vm((G, S, E), BF16),
            vm((N, K), F32),
            vm((N, K), BF16),
            vm((2, K // 2, N), BF16),
            vm((2, K // 2, E // 2), F32),
            vm((G, S, K), BF16),
            vm((tok, 1), jnp.int32),
            vm((G, 8, 128), F32),
            vm((R, -(-G // 8) * 8, 128), F32),
            vm((G, K, 128), F32),
            vm((2, R, 1, K), F32),
            vm((M, Z * QM, E), BF16),
            vm((2, M, Z * QM, E), BF16),
            vm((M, Z, QM, E), BF16),
            vm((2, M, Z, QM, E), BF16),
            vm((2, 2, M, Z, QM, E), BF16),
            dma((tok // x_sem_rows(tok),)), dma, dma,
            dma((G * per,)), dma((G * per,)),
            dma((G,)), dma((G,)),
            dma((R,)), dma((R,)),
            dma((2, R)), dma((2, R)),
            dma((2, M)), dma((2, M)),
            dma((2, M, Z)), dma((2, M, Z)),
            dma((2, M, Z)), dma((2, M, Z)),
            dma((2, M, Z)), dma((2, M, Z)),
            dma((G,)), dma((G,)),
        ],
        compiler_params=pltpu.CompilerParams(
            collective_id=0, has_side_effects=True, vmem_limit_bytes=48 * 1024 * 1024,
        ),
    )(*[pltpu.with_memory_space_constraint(v, pltpu.HBM) for v in (embeddings, labels.reshape(1, tok), init_idx)])
    return (assign, means[None])


def solution(mesh):
    return jax.shard_map(
        functools.partial(on_device, mesh.shape["sc"], mesh.shape["rows"]),
        mesh=mesh,
        in_specs=(P(("sc", "rows"), None), P(("sc", "rows"), None), P("sc", None)),
        out_specs=(P(("sc", "rows"), None), P("sc", None, None)),
        check_vma=False,
    )
```

```python
import functools
import math

import jax
import jax.numpy as jnp
from jax import lax
from jax.experimental import pallas as pl
from jax.experimental.pallas import tpu as pltpu
from jax.sharding import PartitionSpec as P

ITERS = 3
ROUNDS = 3
MESH = pl.DeviceIdType.MESH
F32 = jnp.float32
BF16 = jnp.bfloat16


def x_sem_rows(tok):
    return min(256, tok)


def flip(i, bits):
    for b in range(bits.bit_length()):
        if bits >> b & 1:
            i = i + (1 << b) - (i // (1 << b) % 2) * (2 << b)
    return i


def cut(first, last, size):
    return [(at, min(size, last - at)) for at in range(first, last, size)]


def kernel(
    G, R, tok, E, K, S, T, A, pieces, early_pieces,
    x_ref, labr_hbm, init_hbm,
    assign_ref, means_ref,
    labr_ref, init_ref, xin, xu, out, inc, plan, planb, lhst, acc, ret, target,
    msg, tab, tall, cs, s1s, s1r, s2s, s2r, cent,
    x_sem, l_sem, i_sem, d_ss, d_rs, c_ss, c_rs, k_ss, k_rs, cs_ss, cs_rs,
    s1_ss, s1_rs, s2_ss, s2_rs, g_ss, g_rs, f_ss, f_rs, r_ss, r_rs,
):
    g = lax.axis_index("sc")
    r = lax.axis_index("rows")
    Z = R // 2
    H = K // 2
    Q = H // Z
    M = 2 if Q % 32 == 0 else 1
    QM = Q // M
    N = G * S
    GP = -(-G // 8) * 8
    F = pieces[early_pieces - 1][0] + pieces[early_pieces - 1][1]
    per = len(pieces)
    XT = x_sem_rows(tok)
    z = r // 2
    c = r % 2
    half = (c + z) % 2
    oc = 1 - half
    partner = z * 2 + 1 - c

    def copy(src, dst, ss, rs, to):
        return pltpu.make_async_remote_copy(
            src_ref=src, dst_ref=dst, send_sem=ss, recv_sem=rs,
            device_id=to, device_id_type=MESH,
        )

    barrier = pltpu.get_barrier_semaphore()
    for off in range(1, R):
        pl.semaphore_signal(barrier, inc=1, device_id=(g, (r + off) % R), device_id_type=MESH)
    for off in range(1, G):
        pl.semaphore_signal(barrier, inc=1, device_id=((g + off) % G, r), device_id_type=MESH)

    small = [
        pltpu.make_async_copy(labr_hbm, labr_ref, l_sem),
        pltpu.make_async_copy(init_hbm, init_ref, i_sem),
    ]
    for d in small:
        d.start()
    for i in range(tok // XT):
        at = pl.ds(i * XT, XT)
        pltpu.make_async_copy(x_ref.at[at, :], xin.at[at, :], x_sem.at[i]).start()
    for d in small:
        d.wait()

    lanes = lax.broadcasted_iota(jnp.int32, (1, 128), 1)
    sub = lax.broadcasted_iota(jnp.int32, (128, 128), 0)
    lane = lax.broadcasted_iota(jnp.int32, (128, 128), 1)
    tri = jnp.where(sub < lane, 1.0, 0.0).astype(BF16)
    labr = labr_ref[...]
    mem = jnp.where(lax.broadcasted_iota(jnp.int32, (16, tok), 0) == labr, 1.0, 0.0)

    def before(marks):
        seen = jnp.zeros((16, 1), F32)
        places = []
        for b in range(tok // 128):
            part = marks[:, b * 128:(b + 1) * 128]
            ahead = jnp.dot(part.astype(BF16), tri, preferred_element_type=F32) + seen
            places.append(jnp.sum(ahead * mem[:, b * 128:(b + 1) * 128], axis=0, keepdims=True))
            seen = seen + jnp.sum(part, axis=1, keepdims=True)
        return jnp.concatenate(places, axis=1), seen

    held = jnp.sum(mem, axis=1, keepdims=True)
    msg[g] = jnp.zeros((8, 128), F32)
    msg[g, 0:1, :] = jnp.sum(jnp.where(sub[:16] == lane[:16], held, 0.0), axis=0, keepdims=True)
    for i in range(K // 128):
        msg[g, 1 + i:2 + i, :] = init_ref[:, i * 128:(i + 1) * 128].astype(F32)

    pl.semaphore_wait(barrier, R - 1 + G - 1)

    count_sends = []
    for off in range(1, G):
        d = copy(msg.at[g], msg.at[g], c_ss.at[off], c_rs.at[g], ((g + off) % G, r))
        d.start()
        count_sends.append(d)

    for i in range(tok // XT):
        at = pl.ds(i * XT, XT)
        pltpu.make_async_copy(x_ref.at[at, :], xin.at[at, :], x_sem.at[i]).wait()
        v = xin[at, :].astype(F32)
        scale = lax.rsqrt(jnp.mean(v * v, axis=1, keepdims=True) + 1e-05) * (1.0 / math.sqrt(E))
        xu[at, :] = (v * scale).astype(BF16)

    place, _ = before(mem)
    row_sends = []

    def moved(chosen, start, size):
        slot = lax.broadcasted_iota(jnp.int32, (size, tok), 0) + start
        perm = jnp.concatenate([jnp.where(slot == one, 1.0, 0.0).astype(BF16) for one in chosen], axis=0)
        return jnp.dot(perm, xu[...], preferred_element_type=F32).astype(BF16)

    def send_piece(j, chosen):
        start, size = pieces[j]
        at = pl.ds(start, size)
        block = moved(chosen, start, size)
        for off in range(1, G):
            out[off - 1, at, :] = block[(off - 1) * size:off * size]
            d = copy(
                out.at[off - 1, at, :], inc.at[g, at, :],
                d_ss.at[off * per + j], d_rs.at[g * per + j], ((g + off) % G, r),
            )
            d.start()
            row_sends.append(d)

    def wait_piece(j):
        for off in range(1, G):
            src = (g + off) % G
            part = inc.at[src, pl.ds(*pieces[j]), :]
            copy(part, part, d_ss.at[off * per + j], d_rs.at[src * per + j], (src, r)).wait_recv()

    def chosen_of(place_i):
        return [jnp.where(labr == (g + off) % G, place_i, -1) for off in range(1, G + 1)]

    send_piece(0, chosen_of(place.astype(jnp.int32))[:G - 1])

    for off in range(1, G):
        src = (g + off) % G
        copy(msg.at[src], msg.at[src], c_ss.at[off], c_rs.at[src], (src, r)).wait_recv()
    tab[r] = jnp.zeros((GP, 128), F32)
    for q in range(G):
        tab[r, q:q + 1, :] = msg[q, 0:1, :]
    rank_sends = []
    for off in range(1, R):
        to = (r + off) % R
        d = copy(tab.at[r], tab.at[r], k_ss.at[off], k_rs.at[r], (g, to))
        d.start()
        rank_sends.append(d)
    def asked_of(q):
        return jnp.concatenate([msg[q, 1 + i:2 + i, :] for i in range(K // 128)], axis=1)

    for q in range(G):
        tall[q] = jnp.broadcast_to(asked_of(q), (128, K)).T
    for off in range(1, R):
        src = (r + off) % R
        copy(tab.at[src], tab.at[src], k_ss.at[off], k_rs.at[src], (g, src)).wait_recv()
    totals = jnp.zeros((GP, 128), F32)
    early = jnp.zeros((GP, 128), F32)
    for q in range(R):
        rows = tab[q]
        totals = totals + rows
        early = early + jnp.where(r > q, rows, 0.0)
    total = jnp.sum(totals, axis=0, keepdims=True)
    where_g = lax.broadcasted_iota(jnp.int32, (GP, 128), 0)
    ahead = jnp.sum(
        jnp.where(where_g < g, totals, 0.0) + jnp.where(where_g == g, early, 0.0), axis=0, keepdims=True
    )

    def at_lane(row, q):
        return jnp.sum(jnp.where(lanes == q, row, 0.0), axis=1, keepdims=True)

    def wanted_of(q, asked):
        count = at_lane(total, q)
        return asked - jnp.floor((asked + 0.5) / count) * count

    span = 2.0 * G * R * S
    key = place
    for q in range(G):
        key = key + jnp.where(labr == q, at_lane(ahead, q) + q * span, 0.0)
    hits = jnp.zeros((8, tok), F32)
    for q in range(G):
        goal = wanted_of(q, tall[q]) + q * span
        hits = hits + jnp.concatenate([
            jnp.sum(
                jnp.where(goal == key[:, b * 128:(b + 1) * 128], 1.0, 0.0).reshape(K // 8, 8, 128), axis=0
            )
            for b in range(tok // 128)
        ], axis=1)
    hit = (jnp.sum(hits, axis=0, keepdims=True) > 0.0) & (place >= A)
    seeds = jnp.where(hit, mem, 0.0)
    seed_place, seed_count = before(seeds)
    seeds_all = jnp.sum(seed_count * mem, axis=0, keepdims=True)
    place = jnp.where(
        place < A, place, jnp.where(hit, seed_place + A, place + seeds_all - seed_place)
    )
    chosen = chosen_of(place.astype(jnp.int32))
    for j in range(1, per):
        send_piece(j, chosen[:G - 1])
    for i in range(S // T):
        inc[g, pl.ds(i * T, T), :] = moved(chosen[G - 1:], i * T, T)

    slot_of = labr.astype(F32) * S + place
    for b in range(tok // 128):
        wide = jnp.broadcast_to(slot_of[:, b * 128:(b + 1) * 128], (128, 128))
        target[pl.ds(b * 128, 128), :] = wide.T[:, :1].astype(jnp.int32)

    mine = jnp.where(lax.broadcasted_iota(jnp.int32, (GP, 128), 1) == g, 1.0, 0.0)
    totals_g = jnp.sum(totals * mine, axis=1, keepdims=True)
    early_g = jnp.sum(early * mine, axis=1, keepdims=True)
    here_g = jnp.sum(tab[r] * mine, axis=1, keepdims=True)
    n_here = [here_g[q:q + 1] for q in range(G)]
    wide_w = wanted_of(g, asked_of(g))
    tall_w = wanted_of(g, tall[g])[:, :1]
    before_k = lax.broadcasted_iota(jnp.int32, (K, K), 0) < lax.broadcasted_iota(jnp.int32, (K, K), 1)
    again = jnp.max(jnp.where((tall_w == wide_w) & before_k, 1.0, 0.0), axis=0, keepdims=True)
    lower = jnp.sum(jnp.where(wide_w < tall_w, 1.0 - again, 0.0), axis=1, keepdims=True)
    slots = lax.broadcasted_iota(jnp.int32, (1, F), 1).astype(F32)
    base = jnp.zeros((1, 1), F32)
    for q in range(G):
        start = base + early_g[q:q + 1]
        base = base + totals_g[q:q + 1]
        local = tall_w - start
        fewer = jnp.sum(jnp.where(wide_w < start + A, 1.0 - again, 0.0), axis=1, keepdims=True)
        slot = jnp.where(local < A, local, lower - fewer + A)
        slot = jnp.where((local >= 0.0) & (local < n_here[q]), slot, -1.0)
        pick = jnp.where(slot == slots, 1.0, 0.0).astype(BF16)
        lhst[0, :, pl.ds(q * S, F)] = pick[:H]
        lhst[1, :, pl.ds(q * S, F)] = pick[H:]

    for j in range(early_pieces):
        wait_piece(j)

    C = E // 2
    pending = []

    def half_sum(h, e):
        rows = inc[:, :, pl.ds(e * C, C)].reshape(N, C)
        return jnp.dot(lhst[h], rows, preferred_element_type=F32)

    def seed_sum(h, e):
        total = None
        for q in range(G):
            part = jnp.dot(
                lhst[h, :, pl.ds(q * S, F)], inc[q, pl.ds(0, F), pl.ds(e * C, C)],
                preferred_element_type=F32,
            )
            total = part if total is None else total + part
        return total

    def big(t, finish, theirs, meanwhile=None, half_sum=half_sum):
        slot = t % 2
        first = []
        sends = []
        for m in range(M):
            for e in range(2):
                s1s[m, :, pl.ds(e * C, C)] = theirs[e][m * Z * QM:(m + 1) * Z * QM].astype(BF16)
            d = copy(s1s.at[m], s1r.at[slot, m], s1_ss.at[slot, m], s1_rs.at[slot, m], (g, partner))
            d.start()
            first.append(d)
        for e in range(2):
            acc[e] = half_sum(half, e)
        for m in range(M):
            at = pl.ds(m * Z * QM, Z * QM)
            first[m].wait_recv()
            for e in range(2):
                both = acc[e, at, :] + s1r[slot, m, :, pl.ds(e * C, C)].astype(F32)
                acc[e, at, :] = both
                s2s[m, :, :, pl.ds(e * C, C)] = both.astype(BF16).reshape(Z, QM, C)
            for off in range(Z - 1, 0, -1):
                to = flip(z, off)
                d = copy(
                    s2s.at[m, to], s2r.at[slot, m, z],
                    s2_ss.at[slot, m, off], s2_rs.at[slot, m, z], (g, to * 2 + (half + to) % 2),
                )
                d.start()
                sends.append(d)
        for m in range(M):
            at = pl.ds(pl.multiple_of(m * Z * QM + z * QM, QM), QM)
            own = jnp.concatenate([acc[0, at, :], acc[1, at, :]], axis=1)
            for off in range(Z - 1, 0, -1):
                src = flip(z, off)
                part = s2r.at[slot, m, src]
                copy(
                    part, part, s2_ss.at[slot, m, off], s2_rs.at[slot, m, src], (g, src * 2 + (half + src) % 2)
                ).wait_recv()
                own = own + s2r[slot, m, src].astype(F32)
            mine = cent.at[slot, half, m, z]
            cent[slot, half, m, z] = finish(own, m).astype(BF16)
            for off in range(Z - 1, 0, -1):
                to = flip(z, off)
                d = copy(mine, mine, g_ss.at[slot, m, off], g_rs.at[slot, m, z], (g, to * 2 + (half + to) % 2))
                d.start()
                sends.append(d)
            d = copy(mine, mine, f_ss.at[slot, m, z], f_rs.at[slot, m, z], (g, partner))
            d.start()
            sends.append(d)
        if meanwhile is not None:
            meanwhile()
        for m in range(M):
            for off in range(Z - 1, 0, -1):
                src = flip(z, off)
                part = cent.at[slot, half, m, src]
                copy(part, part, g_ss.at[slot, m, off], g_rs.at[slot, m, src], (g, src * 2 + (half + src) % 2)).wait_recv()
                d = copy(part, part, f_ss.at[slot, m, src], f_rs.at[slot, m, src], (g, partner))
                d.start()
                sends.append(d)
        for m in range(M):
            for off in range(Z):
                src = flip(z, off)
                part = cent.at[slot, oc, m, src]
                copy(part, part, f_ss.at[slot, m, src], f_rs.at[slot, m, src], (g, partner)).wait_recv()
        pending.extend(first + sends)

    def column_start(t, part8):
        slot = t % 2
        cs[slot, r] = jnp.sum(part8, axis=0, keepdims=True)
        sends = []
        for off in sorted(range(1, R), key=lambda o: -min(o, R - o)):
            to = (r + off) % R
            d = copy(cs.at[slot, r], cs.at[slot, r], cs_ss.at[slot, off], cs_rs.at[slot, r], (g, to))
            d.start()
            sends.append(d)
        for d in pending:
            d.wait_send()
        pending[:] = sends
        return sends

    def column_sum(t, sends):
        slot = t % 2
        for off in range(1, R):
            src = (r + off) % R
            part = cs.at[slot, src]
            copy(part, part, cs_ss.at[slot, off], cs_rs.at[slot, src], (g, src)).wait_recv()
        whole = cs[slot, 0]
        for q in range(1, R):
            whole = whole + cs[slot, q]
        return whole

    tiles = N // T
    zero8 = jnp.zeros((8, K), F32)

    def down(v):
        return jnp.sum(v.reshape(v.shape[0] // 8, 8, K), axis=0)

    def assign_rows():
        for off in range(1, G):
            src = (g + off) % G
            part = ret.at[src]
            copy(part, part, r_ss.at[off], r_rs.at[src], (src, r)).wait_recv()

        def one(i, carry):
            at = pl.ds(pl.multiple_of(i * 256, 256), 256)
            hot = jnp.where(
                lax.broadcasted_iota(jnp.int32, (256, N), 1) == target[at, :], 1.0, 0.0
            ).astype(BF16)
            assign_ref[at, :] = jnp.dot(
                hot, ret[...].reshape(N, K), preferred_element_type=F32
            ).astype(BF16)
            return carry

        lax.fori_loop(0, tok // 256, one, 0)

    big(0, lambda v, m: v, [seed_sum(oc, e) for e in range(2)], None, seed_sum)
    step = 0
    back_sends = []
    for round_index in range(ROUNDS):
        last = round_index == ROUNDS - 1
        slot = round_index % 2
        part = zero8
        areas = [(0, F)] + [(F, S - F)] * (F < S) if round_index == 0 else [(0, S)]
        for j, (start, size) in enumerate(areas):
            if round_index == 0 and j > 0:
                for piece in range(early_pieces, per):
                    wait_piece(piece)
            for q in range(G):
                v = lax.dot_general(
                    inc[q, pl.ds(start, size), :], cent[slot].reshape(K, E),
                    (((1,), (1,)), ((), ())), preferred_element_type=F32,
                )
                at = (lax.broadcasted_iota(jnp.int32, (size, 1), 0) + start).astype(F32)
                v = jnp.where(at < n_here[q], jnp.exp(v * 10.0), 0.0)
                plan[pl.ds(q * S + start, size), :] = v
                part = part + down(v)
        for it in range(ITERS):
            col = 1.0 / column_sum(step, column_start(step, part))
            step += 1
            part = zero8
            if it < ITERS - 1:
                for i in range(tiles):
                    v = plan[pl.ds(i * T, T), :]
                    s = jnp.sum(v * col, axis=1, keepdims=True)
                    part = part + down(v * jnp.where(s > 0.0, 1.0 / s, 0.0))
            else:
                theirs = [None, None]
                for q in range(G):
                    at = pl.ds(q * S, S)
                    v = plan[at, :] * col
                    s = jnp.sum(v, axis=1, keepdims=True)
                    v = v * jnp.where(s > 0.0, 1.0 / s, 0.0)
                    if last:
                        planb[at, :] = v.astype(BF16)
                        part = part + down(v)
                    vt = v.T.astype(BF16)
                    lhst[0, :, at] = vt[:H]
                    lhst[1, :, at] = vt[H:]
                    vo = jnp.where(half == 0, vt[H:], vt[:H])
                    for e in range(2):
                        d = jnp.dot(vo, inc[q, :, pl.ds(e * C, C)], preferred_element_type=F32)
                        theirs[e] = d if theirs[e] is None else theirs[e] + d
        if not last:
            big(
                round_index + 1,
                lambda v, m: v * lax.rsqrt(jnp.sum(v * v, axis=1, keepdims=True) + 1e-06),
                theirs,
            )
        else:
            for off in range(1, G):
                to = (g + off) % G
                d = copy(
                    planb.at[pl.ds(pl.multiple_of(to * S, S), S), :], ret.at[g],
                    r_ss.at[off], r_rs.at[g], (to, r),
                )
                d.start()
                back_sends.append(d)
            ret[g] = planb[pl.ds(pl.multiple_of(g * S, S), S), :]
            weight_sends = column_start(step, part)
            weights = []

            def mean_of(v, m):
                if m == 0:
                    weights.append(column_sum(step, weight_sends))
                wide = lax.broadcasted_iota(jnp.int32, (QM, K), 0) + (half * H + m * Z * QM + z * QM)
                pick = wide == lax.broadcasted_iota(jnp.int32, (QM, K), 1)
                return v / jnp.sum(jnp.where(pick, weights[0], 0.0), axis=1, keepdims=True)

            big(ROUNDS, mean_of, theirs, assign_rows)
            means_ref[...] = cent[ROUNDS % 2].reshape(K, E).astype(F32)

    for d in pending + count_sends + row_sends + rank_sends + back_sends:
        d.wait_send()


def on_device(G, R, embeddings, labels, init_idx):
    tok, E = embeddings.shape
    K = init_idx.shape[1]
    S = 2 * tok // G
    T = min(256, S)
    N = G * S
    Z = R // 2
    Q = K // 2 // Z
    M = 2 if Q % 32 == 0 else 1
    QM = Q // M
    A = min(64, S)
    F = min(S, A + K)
    early = [(0, A)] + cut(A, F, 128)
    pieces = early + cut(F, S, 128)
    per = len(pieces)
    dma = pltpu.SemaphoreType.DMA
    vm = pltpu.VMEM
    assign, means = pl.pallas_call(
        functools.partial(kernel, G, R, tok, E, K, S, T, A, pieces, len(early)),
        out_shape=(
            jax.ShapeDtypeStruct((tok, K), BF16),
            jax.ShapeDtypeStruct((K, E), F32),
        ),
        in_specs=[pl.BlockSpec(memory_space=pltpu.HBM)] * 3,
        out_specs=[pl.BlockSpec(memory_space=pltpu.VMEM)] * 2,
        scratch_shapes=[
            vm((1, tok), jnp.int32),
            vm((1, K), jnp.int32),
            vm((tok, E), BF16),
            vm((tok, E), BF16),
            vm((G - 1, S, E), BF16),
            vm((G, S, E), BF16),
            vm((N, K), F32),
            vm((N, K), BF16),
            vm((2, K // 2, N), BF16),
            vm((2, K // 2, E // 2), F32),
            vm((G, S, K), BF16),
            vm((tok, 1), jnp.int32),
            vm((G, 8, 128), F32),
            vm((R, -(-G // 8) * 8, 128), F32),
            vm((G, K, 128), F32),
            vm((2, R, 1, K), F32),
            vm((M, Z * QM, E), BF16),
            vm((2, M, Z * QM, E), BF16),
            vm((M, Z, QM, E), BF16),
            vm((2, M, Z, QM, E), BF16),
            vm((2, 2, M, Z, QM, E), BF16),
            dma((tok // x_sem_rows(tok),)), dma, dma,
            dma((G * per,)), dma((G * per,)),
            dma((G,)), dma((G,)),
            dma((R,)), dma((R,)),
            dma((2, R)), dma((2, R)),
            dma((2, M)), dma((2, M)),
            dma((2, M, Z)), dma((2, M, Z)),
            dma((2, M, Z)), dma((2, M, Z)),
            dma((2, M, Z)), dma((2, M, Z)),
            dma((G,)), dma((G,)),
        ],
        compiler_params=pltpu.CompilerParams(
            collective_id=0, has_side_effects=True, vmem_limit_bytes=48 * 1024 * 1024,
        ),
    )(*[pltpu.with_memory_space_constraint(v, pltpu.HBM) for v in (embeddings, labels.reshape(1, tok), init_idx)])
    return (assign, means[None])


def solution(mesh):
    return jax.shard_map(
        functools.partial(on_device, mesh.shape["sc"], mesh.shape["rows"]),
        mesh=mesh,
        in_specs=(P(("sc", "rows"), None), P(("sc", "rows"), None), P("sc", None)),
        out_specs=(P(("sc", "rows"), None), P("sc", None, None)),
        check_vma=False,
    )
```
